32 devices in a mesh: rep: 8 (over z, y), shard: 4 (over x, core).
Axes of the slice: x: 2, y: 2, z: 4, core: 2. Of those that a mesh axis runs over, the one named last changes fastest.
Arguments:
- images: bfloat16 [32, 8, 32, 640], P(('rep', 'shard')), may hold values from -6 to 6
- conv_weight: bfloat16 [5760, 640], P('shard'), may hold values from -0.078125 to 0.078125
- skip_weight: bfloat16 [640, 1280], P('shard'), may hold values from -0.25 to 0.25
- cotangent: bfloat16 [32, 4, 16, 1280], P(('rep', 'shard')), may hold values from -6 to 6
- hidden_cot: bfloat16 [32, 8, 32, 640], P(('rep', 'shard')), may hold values from -6 to 6
Outputs:
- hidden: bfloat16 [32, 8, 32, 640], P(('rep', 'shard'))
- projected: bfloat16 [32, 4, 16, 1280], P(('rep', 'shard'))
- input_grad: bfloat16 [32, 8, 32, 640], P(('rep', 'shard'))
- conv_grad: float32 [5760, 640], P('shard')
- skip_grad: float32 [640, 1280], P('shard')
The draws below stay inside these ranges and needn't reach their ends.
All inputs are finite; a program needn't handle non-finite values.
Results may differ from the reference program's by a relative error of at most 0.0052.
Values may be sent and summed in bfloat16 or wider, within the bound.
No kernel may reach another device: no remote copies, remote signals or barrier semaphores. Data moves between devices by JAX's collectives and lax.ppermute only.
A program may use at most 128 MiB of HBM per device.

```python
import math
import jax
import jax.numpy as jnp
from jax import lax

C = 640
CO = 1280
HT = 8
WD = 32
IMAGES = 32


def steps_of(own_key, dims, cuts, low, largest):
    level, own = 1.0, jax.random.fold_in(own_key, 6)
    for dim, shards_of in cuts:
        steps = jnp.exp(jax.random.uniform(jax.random.fold_in(own, dim), (shards_of,), jnp.float32, low / len(cuts), largest / len(cuts)))
        level = level * jnp.repeat(steps, dims[dim] // shards_of).reshape([-1 if axis == dim else 1 for axis in range(len(dims))])
    return level


def normal_values(rng, extent, scale, reach, cuts=(), kind=jnp.bfloat16):
    entries = jax.random.normal(rng, extent, jnp.float32) * scale
    if len(cuts) > 0:
        entries = steps_of(rng, extent, cuts, -0.22, 0.18) * entries
    return jnp.clip(entries, min=-reach, max=reach).astype(kind)


def setup_inputs(seed: int = 0) -> dict:
    keys = jax.random.split(jax.random.key(seed), 6)
    images = normal_values(keys[0], (IMAGES, HT, WD, C), 1.0, 6.0, ((0, 32),))
    conv_weight = normal_values(keys[1], (9 * C, C), (9 * C) ** -0.5, 0.078125, ((0, 4),))
    skip_weight = normal_values(keys[2], (C, CO), C ** -0.5, 0.25, ((0, 4),))
    cotangent = normal_values(keys[3], (IMAGES, HT // 2, WD // 2, CO), 1.0, 6.0, ((0, 32),))
    hidden_cot = normal_values(keys[4], (IMAGES, HT, WD, C), 1.0, 6.0, ((0, 32),))
    return {"images": images, "conv_weight": conv_weight, "skip_weight": skip_weight, "cotangent": cotangent, "hidden_cot": hidden_cot}


def columns(activated):
    height, width_cells, channels = activated.shape
    padded = jnp.pad(activated, ((1, 1), (1, 1), (0, 0)))
    shifts = [padded[row_off:row_off + height, col_off:col_off + width_cells, :] for row_off in range(3) for col_off in range(3)]
    return jnp.stack(shifts, axis=-1).reshape(height * width_cells, channels * 9)

def scatter_back(pieces):
    height, width_cells = (pieces.shape[0], pieces.shape[1])
    running = jnp.zeros((height + 2, width_cells + 2, pieces.shape[2]), jnp.float32)
    for row_off in range(3):
        for col_off in range(3):
            running = running + jnp.pad(pieces[..., row_off * 3 + col_off], ((row_off, 2 - row_off), (col_off, 2 - col_off), (0, 0)))
    return running[1:-1, 1:-1]

def spread_even(back_sub):
    blanks = jnp.zeros_like(back_sub)
    half_rows, half_cols, channels = back_sub.shape
    rowwise = jnp.stack([back_sub, blanks], axis=2).reshape(half_rows, 2 * half_cols, channels)
    return jnp.stack([rowwise, jnp.zeros_like(rowwise)], axis=1).reshape(2 * half_rows, 2 * half_cols, channels)

def reference(images, conv_weight, skip_weight, cotangent, hidden_cot):
    number_images, height, width_cells, channels = images.shape
    wide_chans = skip_weight.shape[1]

    def per_image(partial_value, inputs_triple):
        source, grad_out, grad_hidden = inputs_triple
        source_f = source.astype(jnp.float32)
        activated = jax.nn.silu(source_f).astype(jnp.bfloat16)
        patches = columns(activated)
        convolved = jnp.dot(patches, conv_weight, preferred_element_type=jnp.float32).reshape(height, width_cells, channels)
        hidden = (source_f + convolved).astype(jnp.bfloat16)
        subsampled = hidden[::2, ::2].reshape(-1, channels)
        grad_rows = grad_out.reshape(-1, wide_chans)
        projected = jnp.dot(subsampled, skip_weight, preferred_element_type=jnp.float32).astype(jnp.bfloat16).reshape(grad_out.shape)
        skip_term = jnp.dot(subsampled.T, grad_rows, preferred_element_type=jnp.float32)
        back_sub = jnp.dot(grad_rows, skip_weight.T, preferred_element_type=jnp.float32).astype(jnp.bfloat16)
        spread = spread_even(back_sub.reshape(height // 2, width_cells // 2, channels))
        hidden_grad = (grad_hidden.astype(jnp.float32) + spread.astype(jnp.float32)).astype(jnp.bfloat16)
        hidden_flat = hidden_grad.reshape(-1, channels)
        conv_term = jnp.dot(patches.T, hidden_flat, preferred_element_type=jnp.float32)
        tap_grads = jnp.dot(hidden_flat, conv_weight.T, preferred_element_type=jnp.float32)
        input_side = scatter_back(tap_grads.reshape(height, width_cells, channels, 9))
        sigmoid = jax.nn.sigmoid(source_f)
        slope = sigmoid * (1.0 + source_f * (1.0 - sigmoid))
        input_grad = (hidden_grad.astype(jnp.float32) + slope * input_side).astype(jnp.bfloat16)
        return ((partial_value[0] + conv_term, partial_value[1] + skip_term), (hidden, projected, input_grad))
    initial = (jnp.zeros(conv_weight.shape, jnp.float32), jnp.zeros(skip_weight.shape, jnp.float32))
    sums, outputs = lax.scan(per_image, initial, (images, cotangent, hidden_cot))
    grad_factor = 1.0 / math.sqrt(number_images * (height // 2) * (width_cells // 2))
    return (outputs[0], outputs[1], outputs[2], sums[0] * grad_factor, sums[1] * grad_factor)
```

```python
import functools
import math

import jax
import jax.numpy as jnp
from jax import lax
from jax.experimental import pallas as pl
from jax.experimental.pallas import tpu as pltpu
from jax.sharding import PartitionSpec as P

BF = jnp.bfloat16
F32 = jnp.float32
VMEM_LIMIT = 48 << 20
LANES = 128


def dot(a, b, dims):
    return lax.dot_general(a, b, (dims, ((), ())), preferred_element_type=F32)


def call(body, outs, scratch, flops, moved, *args, smem=()):
    specs = [
        pl.BlockSpec(memory_space=pltpu.SMEM if i in smem else pltpu.VMEM)
        for i in range(len(args))
    ]
    return pl.pallas_call(
        body,
        out_shape=outs,
        in_specs=specs,
        out_specs=jax.tree.map(lambda _: pl.BlockSpec(memory_space=pltpu.VMEM), outs),
        scratch_shapes=scratch,
        compiler_params=pltpu.CompilerParams(vmem_limit_bytes=VMEM_LIMIT),
        cost_estimate=pl.CostEstimate(flops=flops, bytes_accessed=moved, transcendentals=0),
    )(*args)


def shape(dims, kind):
    return jax.ShapeDtypeStruct(dims, kind)


def tap_major(conv_weight):
    rows, chans = conv_weight.shape
    own = rows // 9

    def body(w_ref, o_ref, wide):
        for k in range(chans // LANES):
            cols = slice(k * LANES, (k + 1) * LANES)
            wide[k] = w_ref[:, cols].astype(F32)
            for t in range(9):
                o_ref[t, :, cols] = wide[k, pl.ds(t, own, stride=9), :].astype(BF)

    return call(
        body,
        shape((9, own, chans), BF),
        [pltpu.VMEM((chans // LANES, rows, LANES), F32)],
        0,
        4 * rows * chans,
        conv_weight,
    )


def column_mask(pixels, width, own, dx):
    x = lax.broadcasted_iota(jnp.int32, (pixels, own), 0) % width
    return x >= 1 if dx == 0 else x <= width - 2


def forward(own_images, w_tap, height, width):
    number, pixels, own = own_images.shape
    chans = w_tap.shape[2]

    def body(img_ref, w_ref, o_ref, s_ref):
        for m in range(number):
            v = img_ref[m].astype(F32)
            act = (v / (1.0 + jnp.exp(-v))).astype(BF).astype(F32)
            for dx in range(3):
                moved = act
                if dx != 1:
                    moved = pltpu.roll(act, (1 - dx) % pixels, 0)
                    moved = jnp.where(column_mask(pixels, width, own, dx), moved, 0.0)
                s_ref[dx, m, 1 : height + 1] = moved.astype(BF).reshape(height, width, own)
                s_ref[dx, m, 0] = jnp.zeros((width, own), BF)
                s_ref[dx, m, height + 1] = jnp.zeros((width, own), BF)
        for m in range(number):
            acc = jnp.zeros((pixels, chans), F32)
            for dy in range(3):
                for dx in range(3):
                    slab = s_ref[dx, m, dy : dy + height].reshape(pixels, own)
                    acc = acc + dot(slab, w_ref[3 * dy + dx], ((1,), (0,)))
            o_ref[m] = acc

    return call(
        body,
        [shape((number, pixels, chans), F32), shape((3, number, height + 2, width, own), BF)],
        [],
        2 * 9 * number * pixels * own * chans,
        number * pixels * chans * 4 + 9 * own * chans * 2,
        own_images,
        w_tap,
    )


def filter_grad(shifted, hidden_grad, total_rows):
    _, number, padded, width, own = shifted.shape
    height = padded - 2
    pixels = height * width
    chans = hidden_grad.shape[2]

    def body(s_ref, h_ref, o_ref):
        hid = h_ref[...].reshape(number * pixels, chans)
        for dy in range(3):
            for dx in range(3):
                t = 3 * dy + dx
                slab = s_ref[dx, :, dy : dy + height].reshape(number * pixels, own)
                o_ref[t * own : (t + 1) * own] = dot(slab, hid, ((0,), (0,)))
        if total_rows > 9 * own:
            o_ref[9 * own :] = jnp.zeros((total_rows - 9 * own, chans), F32)

    return call(
        body,
        shape((total_rows, chans), F32),
        [],
        2 * 9 * number * pixels * own * chans,
        total_rows * chans * 4 + number * pixels * chans * 2,
        shifted,
        hidden_grad,
    )


def image_grad(hidden_grad, own_grad, own_images, w_tap, height, width):
    number, pixels, own = own_images.shape
    chans = w_tap.shape[2]

    def body(h_ref, g_ref, img_ref, w_ref, o_ref, acc):
        for m in range(number):
            acc[...] = jnp.zeros_like(acc)
            hid = h_ref[m]
            for dy in range(3):
                for dx in range(3):
                    part = dot(hid, w_ref[3 * dy + dx], ((1,), (1,)))
                    acc[dx, dy : dy + height] += part.reshape(height, width, own)
            side = acc[1, 1 : height + 1].reshape(pixels, own)
            for dx in (0, 2):
                part = acc[dx, 1 : height + 1].reshape(pixels, own)
                part = pltpu.roll(part, (dx - 1) % pixels, 0)
                side = side + jnp.where(column_mask(pixels, width, own, 2 - dx), part, 0.0)
            v = img_ref[m].astype(F32)
            sig = 1.0 / (1.0 + jnp.exp(-v))
            slope = sig * (1.0 + v * (1.0 - sig))
            o_ref[m] = (g_ref[m].astype(F32) + slope * side).astype(BF)

    return call(
        body,
        shape((number, pixels, own), BF),
        [pltpu.VMEM((3, height + 2, width, own), F32)],
        2 * 9 * number * pixels * own * chans,
        number * pixels * chans * 2 + 9 * own * chans * 2,
        hidden_grad,
        own_grad,
        own_images,
        w_tap,
    )


def pick(pixels, width):
    few = pixels // 4
    row = lax.broadcasted_iota(jnp.int32, (few, pixels), 0)
    col = lax.broadcasted_iota(jnp.int32, (few, pixels), 1)
    half = width // 2
    return (col == (row // half) * (2 * width) + (row % half) * 2).astype(BF)


def add_spread(hidden_cot, back_sub, me, width):
    number, pixels, chans = hidden_cot.shape
    few, own = back_sub.shape[2:]

    def body(me_ref, c_ref, b_ref, o_ref):
        here = me_ref[0]
        one_hot = pick(pixels, width)
        for m in range(number):
            for a in range(number):
                j = here ^ a
                spread = dot(one_hot, b_ref[j, m ^ j], ((0,), (0,)))
                cols = slice(a * own, (a + 1) * own)
                o_ref[m, :, cols] = (c_ref[m, :, cols].astype(F32) + spread).astype(BF)

    return call(
        body,
        shape((number, pixels, chans), BF),
        [],
        2 * number * pixels * few * chans,
        number * pixels * chans * 4,
        me,
        hidden_cot,
        back_sub,
        smem=(0,),
    )


def place_grad(first, second, where, own, scale):
    ranks, rows_a, chans = first.shape
    rows_b = second.shape[1]
    chunk = rows_a + rows_b

    def body(w_ref, a_ref, b_ref, o_ref, wide):
        for c in range(ranks):
            for ref, k, low, rows in ((a_ref, 0, 0, rows_a), (b_ref, 1, rows_a, rows_b)):
                if rows == 0:
                    continue
                start = c * chunk + low
                at = w_ref[k * ranks + c]
                for t in range(9):
                    lo, hi = max(start, t * own), min(start + rows, (t + 1) * own)
                    if lo < hi:
                        piece = ref[at, lo - start : hi - start, :].astype(F32) * scale
                        strided = pl.ds((lo - t * own) * 9 + t, hi - lo, stride=9)
                        for k in range(chans // LANES):
                            wide[k, strided, :] = piece[:, k * LANES : (k + 1) * LANES]
        for k in range(chans // LANES):
            o_ref[:, k * LANES : (k + 1) * LANES] = wide[k]

    return call(
        body,
        shape((9 * own, chans), F32),
        [pltpu.VMEM((chans // LANES, 9 * own, LANES), F32)],
        0,
        9 * own * chans * 6,
        where,
        first,
        second,
        smem=(0,),
    )


def flip(value, axis, bit):
    return lax.ppermute(value, axis, [(i, i ^ bit) for i in range(lax.axis_size(axis))])


def high_bits(count):
    return [1 << k for k in reversed(range(count.bit_length() - 1))]


def gather(value, axis):
    found = {0: value}
    for bit in high_bits(lax.axis_size(axis)):
        for j, held in list(found.items()):
            found[j ^ bit] = flip(held, axis, bit)
    return jnp.stack([found[j] for j in range(len(found))])


def exchange(blocks, axis, me):
    got = []
    for j in range(lax.axis_size(axis)):
        mine = lax.dynamic_index_in_dim(blocks, me ^ j, 0, keepdims=False)
        got.append(flip(mine, axis, j) if j else mine)
    return jnp.stack(got)


def sum_scatter(parts, axis):
    held = {j: parts[j] for j in range(lax.axis_size(axis))}
    for bit in reversed(high_bits(lax.axis_size(axis))):
        keep = [j for j in held if not j & bit]
        send = jnp.stack([held[j ^ bit].astype(BF) for j in keep])
        got = flip(send, axis, bit).astype(F32)
        held = {j: held[j] + got[n] for n, j in enumerate(keep)}
    return held[0]


def sum_everywhere(parts, axis, me, bits):
    count = lax.axis_size(axis)
    depth = count.bit_length() - 1
    held = parts.reshape((2,) * depth + parts.shape[1:])
    left = high_bits(count)
    for bit in bits:
        at = left.index(bit)
        mine = (me // bit) % 2
        send = lax.dynamic_index_in_dim(held, 1 - mine, at, keepdims=False).astype(BF)
        keep = lax.dynamic_index_in_dim(held, mine, at, keepdims=False)
        held = keep + flip(send, axis, bit).astype(F32)
        left.remove(bit)
    done = held.astype(BF)[None]
    order = [0]
    for bit in reversed(bits):
        done = jnp.concatenate([done, flip(done, axis, bit)])
        order = order + [j ^ bit for j in order]
    place = [order.index(j) for j in range(count)]
    where = jnp.asarray(place, jnp.int32)[jnp.arange(count, dtype=jnp.int32) ^ me]
    return done, where


def bit_orders(count):
    up = list(reversed(high_bits(count)))
    return up, up[1::-1] + up[2:]


def round_up(value, step):
    return -(-value // step) * step


def on_device(images, conv_weight, skip_weight, cotangent, hidden_cot):
    _, height, width, chans = images.shape
    own = skip_weight.shape[0]
    wide = skip_weight.shape[1]
    pixels, few = height * width, (height // 2) * (width // 2)
    group, ranks = lax.axis_size("shard"), lax.axis_size("rep")
    me = lax.axis_index("shard").astype(jnp.int32)
    rep = lax.axis_index("rep").astype(jnp.int32)
    me_ref = me.reshape(1)
    source = images.reshape(pixels, chans)

    cots = gather(cotangent.reshape(few, wide), "shard").reshape(group * few, wide)
    blocks = source.reshape(pixels, group, own).transpose(1, 0, 2)
    own_images = exchange(blocks, "shard", me)
    hid_cots = gather(hidden_cot.reshape(pixels, chans), "shard")
    w_tap = tap_major(conv_weight)

    back = dot(cots, skip_weight, ((1,), (1,))).astype(BF)
    backs = gather(back.reshape(group, few, own), "shard")
    hidden_grad = add_spread(hid_cots, backs, me_ref, width)

    partial, shifted = forward(own_images, w_tap, height, width)
    hidden = (source.astype(F32) + sum_scatter(partial, "shard")).astype(BF)

    rows = 9 * own
    chunk = round_up(-(-rows // ranks), 8)
    term = filter_grad(shifted, hidden_grad, chunk * ranks).reshape(ranks, chunk, chans)
    cut = round_up(chunk // 2, 8)
    order_a, order_b = bit_orders(ranks)
    sum_a, where_a = sum_everywhere(term[:, :cut], "rep", rep, order_a)
    sum_b, where_b = sum_everywhere(term[:, cut:], "rep", rep, order_b)
    factor = 1.0 / math.sqrt(ranks * group * few)
    conv_grad = place_grad(sum_a, sum_b, jnp.concatenate([where_a, where_b]), own, factor)

    sub = hidden.reshape(height // 2, 2, width // 2, 2, chans)[:, 0, :, 0].reshape(few, chans)
    sub_blocks = sub.reshape(few, group, own).transpose(1, 0, 2)
    own_subs = exchange(sub_blocks, "shard", me).reshape(group * few, own)
    skip_term = dot(own_subs, cots, ((0,), (0,)))
    halves = 2
    split = skip_term.reshape(ranks // halves, -1, halves, wide // halves).transpose(0, 2, 1, 3)
    split = split.reshape(ranks, -1, wide // halves)
    skip_sum, where_s = sum_everywhere(split, "rep", rep, order_a)
    skip_sum = skip_sum[where_s].reshape(ranks // halves, halves, -1, wide // halves)
    skip_grad = skip_sum.transpose(0, 2, 1, 3).reshape(own, wide).astype(F32) * factor

    skips = gather(skip_weight, "shard")
    skips = skips[jnp.arange(group, dtype=jnp.int32) ^ me].reshape(chans, wide)
    projected = dot(sub, skips, ((1,), (0,))).astype(BF).reshape(cotangent.shape)

    own_grad = lax.dynamic_slice_in_dim(hidden_grad, me * own, own, axis=2)
    own_input = image_grad(hidden_grad, own_grad, own_images, w_tap, height, width)
    got = [own_input[0]] + [flip(own_input[j], "shard", j) for j in range(1, group)]
    got = jnp.stack(got)[jnp.arange(group, dtype=jnp.int32) ^ me]
    input_grad = got.transpose(1, 0, 2).reshape(images.shape)

    return hidden.reshape(images.shape), projected, input_grad, conv_grad, skip_grad


def solution(mesh):
    placed = (
        P(("rep", "shard"), None, None, None),
        P("shard", None),
        P("shard", None),
        P(("rep", "shard"), None, None, None),
        P(("rep", "shard"), None, None, None),
    )
    return jax.shard_map(
        on_device,
        mesh=mesh,
        in_specs=placed,
        out_specs=(
            P(("rep", "shard"), None, None, None),
            P(("rep", "shard"), None, None, None),
            P(("rep", "shard"), None, None, None),
            P("shard", None),
            P("shard", None),
        ),
        check_vma=False,
    )
```

```python
import math

import jax
import jax.numpy as jnp
from jax import lax
from jax.experimental import pallas as pl
from jax.experimental.pallas import tpu as pltpu
from jax.sharding import PartitionSpec as P

BF = jnp.bfloat16
F32 = jnp.float32
VMEM_LIMIT = 56 << 20
LANES = 128
BLOCK = 4


def dot(a, b, dims=((1,), (0,))):
    return lax.dot_general(a, b, (dims, ((), ())), preferred_element_type=F32)


NT = ((1,), (1,))
TN = ((0,), (0,))


def call(name, body, outs, scratch, flops, moved, args, scalars=0):
    specs = [
        pl.BlockSpec(memory_space=pltpu.SMEM if i < scalars else pltpu.VMEM)
        for i in range(len(args))
    ]
    return pl.pallas_call(
        body,
        out_shape=outs,
        in_specs=specs,
        out_specs=jax.tree.map(lambda _: pl.BlockSpec(memory_space=pltpu.VMEM), outs),
        scratch_shapes=scratch,
        compiler_params=pltpu.CompilerParams(vmem_limit_bytes=VMEM_LIMIT),
        cost_estimate=pl.CostEstimate(flops=flops, bytes_accessed=moved, transcendentals=0),
        name=name,
    )(*args)


def shape(dims, kind):
    return jax.ShapeDtypeStruct(dims, kind)


def rows_at(start, size, step):
    return pl.ds(pl.multiple_of(start, step), size)


def round_up(value, step):
    return -(-value // step) * step


def turn_filters(conv_weight):
    rows, chans = conv_weight.shape
    own = rows // 9

    def body(w_ref, o_ref, t_ref, wide):
        for k in range(chans // LANES):
            cols = slice(k * LANES, (k + 1) * LANES)
            wide[k] = w_ref[:, cols].astype(F32)
            for t in range(9):
                piece = wide[k, pl.ds(t, own, stride=9), :]
                o_ref[t * own : (t + 1) * own, cols] = piece.astype(BF)
        t_ref[...] = o_ref[...].T

    return call(
        "turn_filters",
        body,
        [shape((rows, chans), BF), shape((chans, rows), BF)],
        [pltpu.VMEM((chans // LANES, rows, LANES), F32)],
        0,
        6 * rows * chans,
        [conv_weight],
    )


def col_sets(chans):
    rest = (chans - BLOCK * LANES) // BLOCK
    return BLOCK * LANES, rest


def turn_images(ids, source, hidden_cot, group, own):
    pixels, chans = source.shape
    base, rest = col_sets(chans)
    cols = LANES + rest

    def body(id_ref, i_ref, h_ref, img_ref, full_ref, set_ref, wide):
        wide[...] = i_ref[...].astype(F32).T
        for j in range(group):
            img_ref[j] = wide[rows_at((id_ref[0] ^ j) * own, own, 8), :].astype(BF)
        wide[...] = h_ref[...].astype(F32).T
        full_ref[...] = wide[...].astype(BF)
        for k in range(BLOCK):
            q = id_ref[1] ^ k
            set_ref[k, :LANES] = wide[rows_at(q * LANES, LANES, 8), :].astype(BF)
            set_ref[k, LANES:] = wide[rows_at(base + q * rest, rest, 8), :].astype(BF)

    return call(
        "turn_images",
        body,
        [
            shape((group, own, pixels), BF),
            shape((chans, pixels), BF),
            shape((BLOCK, cols, pixels), BF),
        ],
        [pltpu.VMEM((chans, pixels), F32)],
        0,
        10 * pixels * chans,
        [ids, source, hidden_cot],
        1,
    )


def activate(own_images):
    group = number = len(own_images)
    own, pixels = own_images[0].shape[1:]

    def body(*refs):
        for m in range(number):
            v = refs[m][0].astype(F32)
            refs[number][m] = (v / (1.0 + jnp.exp(-v))).astype(BF)

    return call(
        "activate",
        body,
        shape((group, own, pixels), BF),
        [],
        0,
        4 * group * own * pixels,
        own_images,
    )


def back_product(ids, cots, skip_weight):
    few, wide_chans = cots[0].shape
    own = skip_weight.shape[0]
    group = len(cots)

    def body(id_ref, s_ref, *refs):
        o_ref, held = refs[group:]
        for j in range(group):
            held[rows_at((id_ref[0] ^ j) * few, few, 16), :] = refs[j][...]
        o_ref[...] = dot(s_ref[...], held[...], NT).astype(BF)

    return call(
        "back_product",
        body,
        shape((own, group * few), BF),
        [pltpu.VMEM((group * few, wide_chans), BF)],
        2 * own * group * few * wide_chans,
        group * few * wide_chans * 2,
        [ids, skip_weight, *cots],
        1,
    )


def back_sets(ids, backs, chans):
    own, few_all = backs[0].shape
    group = len(backs)
    base, rest = col_sets(chans)

    def body(id_ref, *refs):
        full_ref, set_ref, held = refs[group:]
        for j in range(group):
            held[rows_at((id_ref[0] ^ j) * own, own, 8), :] = refs[j][...].astype(F32)
        full_ref[...] = held[...].astype(BF)
        for k in range(BLOCK):
            q = id_ref[1] ^ k
            set_ref[k, :LANES] = held[rows_at(q * LANES, LANES, 8), :].astype(BF)
            set_ref[k, LANES:] = held[rows_at(base + q * rest, rest, 8), :].astype(BF)

    return call(
        "back_sets",
        body,
        [shape((chans, few_all), BF), shape((BLOCK, LANES + rest, few_all), BF)],
        [pltpu.VMEM((chans, few_all), F32)],
        0,
        6 * chans * few_all,
        [ids, *backs],
        1,
    )


def pixel_parts(pixels, width):
    at = lax.broadcasted_iota(jnp.int32, (1, pixels), 1)
    return at // width, at % width


def neighbours(value, pixels, width):
    height = pixels // width
    y, x = pixel_parts(pixels, width)
    for dy in range(3):
        for dx in range(3):
            off = (dy - 1) * width + dx - 1
            if off == 0:
                yield value
                continue
            inside = (y >= 1 - dy) & (y < height + 1 - dy) & (x >= 1 - dx) & (x < width + 1 - dx)
            yield jnp.where(inside, pltpu.roll(value, -off % pixels, 1), 0.0)


def spread_matrix(few_all, few, pixels, width):
    y, x = pixel_parts(pixels, width)
    coarse = (y // 2) * (width // 2) + x // 2
    even = (y % 2 == 0) & (x % 2 == 0)
    row = lax.broadcasted_iota(jnp.int32, (few_all, pixels), 0)
    for d in range(few_all // few):
        yield jnp.where(even & (row == d * few + coarse), 1.0, 0.0).astype(BF)


def forward(act, w_turned, width):
    group, own, pixels = act.shape
    chans, rows = w_turned.shape

    def body(a_ref, w_ref, keep_ref, send_ref, patch):
        def image(m):
            value = a_ref[m].astype(F32)
            for t, moved in enumerate(neighbours(value, pixels, width)):
                patch[t * own : (t + 1) * own] = moved.astype(BF)
            return dot(w_ref[...], patch[...])

        @pl.loop(0, group // 2)
        def _(i):
            send_ref[i] = image(2 * i + 1).astype(BF)
            keep_ref[i] = image(2 * i)

    return call(
        "forward",
        body,
        [
            shape((group // 2, chans, pixels), F32),
            shape((group // 2, chans, pixels), BF),
        ],
        [pltpu.VMEM((rows, pixels), BF)],
        2 * group * pixels * rows * chans,
        group * chans * pixels * 3,
        [act, w_turned],
    )


def filter_grad(ids, acts, coarse, sets, backs, width, few, cut):
    group = len(sets)
    own, pixels = acts[0].shape[2:]
    cols = sets[0].shape[1]
    few_all = backs[0].shape[1]
    rows = 9 * own
    rest = cols - LANES
    part = round_up(-(-rows // BLOCK), 8)
    n_acts = len(acts)

    def body(id_ref, *refs):
        act_refs = refs[:n_acts]
        set_refs = refs[n_acts : n_acts + group]
        back_refs = refs[n_acts + group : n_acts + group + BLOCK]
        a_out, b_out, act_all, back_all, one_hot, hid, patch, total = refs[-8:]
        for ref, (members, first) in zip(act_refs, coarse):
            for n, k in enumerate(members):
                act_all[k, first : first + ref.shape[1]] = ref[n]
        for k in range(BLOCK):
            back_all[k] = back_refs[k][...]
        for d, matrix in enumerate(spread_matrix(few_all, few, pixels, width)):
            one_hot[d] = matrix
        hid[cols:] = jnp.zeros((hid.shape[0] - cols, group * pixels), BF)
        total[...] = jnp.zeros_like(total)

        @pl.loop(0, BLOCK)
        def _(k):
            for j in range(group):
                here = slice(j * pixels, (j + 1) * pixels)
                spread = dot(back_all[k], one_hot[id_ref[0] ^ j])
                hid[:cols, here] = (set_refs[j][k].astype(F32) + spread).astype(BF)
                value = act_all[k, j].astype(F32)
                for t, moved in enumerate(neighbours(value, pixels, width)):
                    patch[t * own : (t + 1) * own, here] = moved.astype(BF)
            total[...] += dot(patch[...], hid[...], NT)

        last = jnp.zeros((part, LANES), F32)
        for i in range(BLOCK):
            size = min(part, rows - i * part)
            piece = total[i * part : i * part + size, LANES:]
            if size < part:
                piece = jnp.concatenate([piece, jnp.zeros((part - size, LANES), F32)])
            last = last + (pltpu.roll(piece, rest * i, 1) if i else piece)
        a_out[...] = total[:cut, :LANES].astype(BF)
        b_out[: rows - cut] = total[cut:, :LANES].astype(BF)
        b_out[rows - cut :] = last.astype(BF)

    return call(
        "filter_grad",
        body,
        [shape((cut, LANES), BF), shape((rows + part - cut, LANES), BF)],
        [
            pltpu.VMEM((BLOCK, group, own, pixels), BF),
            pltpu.VMEM((BLOCK, cols, few_all), BF),
            pltpu.VMEM((group, few_all, pixels), BF),
            pltpu.VMEM((2 * LANES, group * pixels), BF),
            pltpu.VMEM((rows, group * pixels), BF),
            pltpu.VMEM((rows, 2 * LANES), F32),
        ],
        2 * BLOCK * group * pixels * rows * cols,
        BLOCK * group * pixels * (own + cols) * 2,
        [ids, *acts, *sets, *backs],
        1,
    )


def place_grad(ids, firsts, seconds, own, chans, scale):
    rows = 9 * own
    part = round_up(-(-rows // BLOCK), 8)
    cut = firsts[0][1].shape[1]
    base, rest = col_sets(chans)
    arrays = [array for _, array in firsts + seconds]

    def body(id_ref, *refs):
        o_ref, wide, last = refs[-3:]
        lane = lax.broadcasted_iota(jnp.int32, (part, LANES), 1) // rest

        def store(where, low, piece):
            high = low + piece.shape[0]
            for t in range(9):
                lo, hi = max(low, t * own), min(high, (t + 1) * own)
                if lo < hi:
                    wide[where, pl.ds((lo - t * own) * 9 + t, hi - lo, stride=9), :] = piece[
                        lo - low : hi - low
                    ]

        last[...] = jnp.zeros_like(last)
        for n, (members, _) in enumerate(firsts + seconds):
            first = n < len(firsts)
            for at, k in enumerate(members):
                q = id_ref[1] ^ k
                if first:
                    store(q, 0, refs[n][at].astype(F32) * scale)
                    continue
                store(q, cut, refs[n][at, : rows - cut, :].astype(F32) * scale)
                share = refs[n][at, rows - cut :, :].astype(F32) * scale
                for i in range(BLOCK):
                    turn = ((q - i + BLOCK) % BLOCK) * rest
                    last[i] += jnp.where(lane == q, pltpu.roll(share, turn, 1), 0.0)
        for i in range(BLOCK):
            store(BLOCK, i * part, last[i, : min(part, rows - i * part), :])
        for k in range(chans // LANES):
            o_ref[:, k * LANES : (k + 1) * LANES] = wide[k]

    return call(
        "place_grad",
        body,
        shape((rows, chans), F32),
        [pltpu.VMEM((chans // LANES, rows, LANES), F32), pltpu.VMEM((BLOCK, part, LANES), F32)],
        0,
        rows * chans * 6,
        [ids, *arrays],
        1,
    )


def finish_hidden(ids, source, held, got, group, width):
    pixels, chans = source.shape
    few, own = pixels // 4, chans // group

    def body(id_ref, s_ref, k_ref, g_ref, o_ref, sub_ref, set_ref, wide):
        total = (k_ref[0] + g_ref[0].astype(F32)).T
        hidden = (s_ref[...].astype(F32) + total).astype(BF)
        o_ref[...] = hidden
        (one_hot,) = spread_matrix(few, few, pixels, width)
        sub = dot(one_hot, hidden)
        sub_ref[...] = sub.astype(BF)
        wide[...] = sub.T
        for j in range(group):
            set_ref[j] = wide[rows_at((id_ref[0] ^ j) * own, own, 8), :].astype(BF)

    return call(
        "finish_hidden",
        body,
        [
            shape((pixels, chans), BF),
            shape((few, chans), BF),
            shape((group, own, few), BF),
        ],
        [pltpu.VMEM((chans, few), F32)],
        2 * few * pixels * chans,
        pixels * chans * 10,
        [ids, source, held, got],
        1,
    )


def skip_grad_term(ids, subs, cots):
    own, few = subs[0].shape
    wide_chans = cots[0].shape[1]
    group = len(subs)
    part = own // BLOCK

    def body(id_ref, *refs):
        o_ref, total = refs[-2:]
        term = dot(refs[0][...], refs[group][...])
        for j in range(1, group):
            term = term + dot(refs[j][...], refs[group + j][...])
        for i in range(BLOCK):
            total[i] = term[i * part : (i + 1) * part]
        for k in range(BLOCK):
            o_ref[k] = total[id_ref[1] ^ k]

    return call(
        "skip_grad_term",
        body,
        shape((BLOCK, part, wide_chans), F32),
        [pltpu.VMEM((BLOCK, part, wide_chans), F32)],
        2 * own * few * group * wide_chans,
        own * wide_chans * 4,
        [ids, *subs, *cots],
        1,
    )


def project(sub_sets, skips):
    group, own, few = sub_sets.shape
    wide_chans = skips[0].shape[1]

    def body(s_ref, *refs):
        total = dot(s_ref[0], refs[0][...], TN)
        for j in range(1, group):
            total = total + dot(s_ref[j], refs[j][...], TN)
        refs[group][...] = total.astype(BF)

    return call(
        "project",
        body,
        shape((few, wide_chans), BF),
        [],
        2 * few * group * own * wide_chans,
        group * own * wide_chans * 2,
        [sub_sets, *skips],
    )


def image_grad(ids, cots, back_full, own_images, w_tap, width, few):
    group = len(cots)
    chans, pixels = cots[0].shape
    rows = w_tap.shape[0]
    own = rows // 9
    height = pixels // width
    few_all = back_full.shape[1]

    def body(id_ref, b_ref, w_ref, *refs):
        cot_refs, img_refs = refs[:group], refs[group : 2 * group]
        o_ref, one_hot, hid, tap = refs[2 * group :]
        y, x = pixel_parts(pixels, width)
        for d, matrix in enumerate(spread_matrix(few_all, few, pixels, width)):
            one_hot[d] = matrix
        for j in range(group):
            spread = dot(b_ref[...], one_hot[id_ref[0] ^ j])
            hid[...] = cot_refs[j][...].astype(F32) + spread
            tap[...] = dot(w_ref[...], hid[...].astype(BF))
            side = tap[4 * own : 5 * own]
            for dy in range(3):
                for dx in range(3):
                    off = (dy - 1) * width + dx - 1
                    if off == 0:
                        continue
                    inside = (y >= dy - 1) & (y < height + dy - 1)
                    inside = inside & (x >= dx - 1) & (x < width + dx - 1)
                    t = 3 * dy + dx
                    moved = pltpu.roll(tap[t * own : (t + 1) * own], off % pixels, 1)
                    side = side + jnp.where(inside, moved, 0.0)
            v = img_refs[j][0].astype(F32)
            sig = 1.0 / (1.0 + jnp.exp(-v))
            slope = sig * (1.0 + v * (1.0 - sig))
            mine = hid[rows_at(id_ref[0] * own, own, 8), :].astype(BF).astype(F32)
            o_ref[j] = (mine + slope * side).astype(BF)

    return call(
        "image_grad",
        body,
        shape((group, own, pixels), BF),
        [
            pltpu.VMEM((group, few_all, pixels), BF),
            pltpu.VMEM((chans, pixels), F32),
            pltpu.VMEM((rows, pixels), F32),
        ],
        2 * group * pixels * rows * chans,
        group * pixels * chans * 2,
        [ids, back_full, w_tap, *cots, *own_images],
        1,
    )


def finish_images(ids, pieces, chans):
    group = len(pieces)
    own, pixels = pieces[0].shape[1:]

    def body(id_ref, *refs):
        o_ref, wide = refs[group:]
        for j in range(group):
            wide[rows_at((id_ref[0] ^ j) * own, own, 8), :] = refs[j][0].astype(F32)
        o_ref[...] = wide[...].T.astype(BF)

    return call(
        "finish_images",
        body,
        shape((pixels, chans), BF),
        [pltpu.VMEM((chans, pixels), F32)],
        0,
        pixels * chans * 4,
        [ids, *pieces],
        1,
    )


def flip(value, axis, bit):
    return lax.ppermute(value, axis, [(i, i ^ bit) for i in range(lax.axis_size(axis))])


def after(value, *others):
    return lax.optimization_barrier((value, *others))[0]


def high_bits(count):
    return [1 << k for k in reversed(range(count.bit_length() - 1))]


def gather(value, axis):
    found = {0: value}
    for bit in high_bits(lax.axis_size(axis)):
        for j, held in list(found.items()):
            found[j ^ bit] = flip(held, axis, bit)
    return [found[j] for j in range(len(found))]


def exchange(blocks, axis, count):
    return [flip(blocks[j : j + 1], axis, j) if j else blocks[:1] for j in range(count)]


def both_orders(first, second):
    pairs = []
    for value, bits in ((first, (1, 2)), (second, (2, 1))):
        pair = jnp.stack([value, flip(value, "rep", bits[0])])
        members = (0, bits[0])
        others = tuple(m ^ bits[1] for m in members)
        pairs.append([(members, pair), (others, flip(pair, "rep", bits[1]))])
    return pairs


def add_beyond_block(value):
    for bit in reversed(high_bits(lax.axis_size("rep"))):
        if bit >= BLOCK:
            got = flip(value, "rep", bit)
            value = (value.astype(F32) + got.astype(F32)).astype(BF)
    return value


def sum_scatter(keep, send):
    bits = list(reversed(high_bits(lax.axis_size("shard"))))
    for bit in bits[:-1]:
        total = keep + flip(send, "shard", bit).astype(F32)
        keep, send = total[0::2], total[1::2].astype(BF)
    return keep, flip(send, "shard", bits[-1])


def on_device(images, conv_weight, skip_weight, cotangent, hidden_cot):
    _, height, width, chans = images.shape
    own, wide = skip_weight.shape
    pixels, few = height * width, (height // 2) * (width // 2)
    group, ranks = lax.axis_size("shard"), lax.axis_size("rep")
    ids = jnp.stack([lax.axis_index("shard"), lax.axis_index("rep") % BLOCK]).astype(jnp.int32)
    source = images.reshape(pixels, chans)

    cots = gather(cotangent.reshape(few, wide), "shard")
    img_sets, cot_full, cot_sets = turn_images(
        ids, source, hidden_cot.reshape(pixels, chans), group, own
    )
    own_images = exchange(img_sets, "shard", group)
    cot_sets = jnp.concatenate(exchange(cot_sets, "rep", BLOCK))
    cot_sets = gather(cot_sets, "shard")
    w_tap, w_turned = turn_filters(conv_weight)
    act = activate(own_images)
    half = group // 2
    act_a, act_b = both_orders(act[:half], act[half:])

    backs = gather(back_product(ids, cots, skip_weight), "shard")
    back_full, back_set = back_sets(ids, backs, chans)
    back_set = [piece[0] for piece in exchange(back_set, "rep", BLOCK)]

    rows = 9 * own
    part = round_up(-(-rows // BLOCK), 8)
    cut = round_up((rows + part) // 2, 8)
    coarse = [(members, 0) for members, _ in act_a] + [(members, half) for members, _ in act_b]
    acts = [array for _, array in act_a + act_b]
    term_a, term_b = filter_grad(ids, acts, coarse, cot_sets, back_set, width, few, cut)
    sum_a, sum_b = both_orders(add_beyond_block(term_a), add_beyond_block(term_b))
    factor = 1.0 / math.sqrt(ranks * group * few)
    conv_grad = place_grad(ids, sum_a, sum_b, own, chans, factor)

    keep, send = forward(after(act, back_set[0]), w_turned, width)
    keep, got = sum_scatter(keep, send)
    hidden, _, sub_sets = finish_hidden(ids, source, keep, got, group, width)

    subs = [piece[0] for piece in exchange(sub_sets, "shard", group)]
    term = skip_grad_term(ids, subs, cots)
    term = term[:2] + flip(term[2:].astype(BF), "rep", 2).astype(F32)
    term = (term[0] + flip(term[1].astype(BF), "rep", 1).astype(F32)).astype(BF)
    term = add_beyond_block(term)[None]
    term = jnp.concatenate([term, flip(term, "rep", 1)])
    term = jnp.concatenate([term, flip(term, "rep", 2)])
    term = term[jnp.arange(BLOCK, dtype=jnp.int32) ^ ids[1]]
    skip_grad = term.reshape(own, wide).astype(F32) * factor

    skips = gather(after(skip_weight, back_full), "shard")
    projected = project(sub_sets, skips).reshape(cotangent.shape)

    cot_all = gather(after(cot_full, back_full), "shard")
    own_input = image_grad(
        ids, cot_all, after(back_full, term_a), own_images, w_tap, width, few
    )
    input_grad = finish_images(ids, exchange(own_input, "shard", group), chans)

    return (
        hidden.reshape(images.shape),
        projected,
        input_grad.reshape(images.shape),
        conv_grad,
        skip_grad,
    )


def solution(mesh):
    placed = (
        P(("rep", "shard"), None, None, None),
        P("shard", None),
        P("shard", None),
        P(("rep", "shard"), None, None, None),
        P(("rep", "shard"), None, None, None),
    )
    return jax.shard_map(
        on_device,
        mesh=mesh,
        in_specs=placed,
        out_specs=(
            P(("rep", "shard"), None, None, None),
            P(("rep", "shard"), None, None, None),
            P(("rep", "shard"), None, None, None),
            P("shard", None),
            P("shard", None),
        ),
        check_vma=False,
    )
```

```python
import math

import jax
import jax.numpy as jnp
from jax import lax
from jax.experimental import pallas as pl
from jax.experimental.pallas import tpu as pltpu
from jax.sharding import PartitionSpec as P

BF = jnp.bfloat16
F32 = jnp.float32
VMEM_LIMIT = 56 << 20
LANES = 128
BLOCK = 4


def dot(a, b, dims=((1,), (0,))):
    return lax.dot_general(a, b, (dims, ((), ())), preferred_element_type=F32)


NT = ((1,), (1,))
TN = ((0,), (0,))


def call(name, body, outs, scratch, flops, moved, args, scalars=0):
    specs = [
        pl.BlockSpec(memory_space=pltpu.SMEM if i < scalars else pltpu.VMEM)
        for i in range(len(args))
    ]
    return pl.pallas_call(
        body,
        out_shape=outs,
        in_specs=specs,
        out_specs=jax.tree.map(lambda _: pl.BlockSpec(memory_space=pltpu.VMEM), outs),
        scratch_shapes=scratch,
        compiler_params=pltpu.CompilerParams(vmem_limit_bytes=VMEM_LIMIT),
        cost_estimate=pl.CostEstimate(flops=flops, bytes_accessed=moved, transcendentals=0),
        name=name,
    )(*args)


def shape(dims, kind):
    return jax.ShapeDtypeStruct(dims, kind)


def rows_at(start, size, step):
    return pl.ds(pl.multiple_of(start, step), size)


def round_up(value, step):
    return -(-value // step) * step


def turn_filters(conv_weight):
    rows, chans = conv_weight.shape
    own = rows // 9

    def body(w_ref, o_ref, t_ref, wide):
        for k in range(chans // LANES):
            cols = slice(k * LANES, (k + 1) * LANES)
            wide[k] = w_ref[:, cols].astype(F32)
            for t in range(9):
                piece = wide[k, pl.ds(t, own, stride=9), :]
                o_ref[t * own : (t + 1) * own, cols] = piece.astype(BF)
        t_ref[...] = o_ref[...].T

    return call(
        "turn_filters",
        body,
        [shape((rows, chans), BF), shape((chans, rows), BF)],
        [pltpu.VMEM((chans // LANES, rows, LANES), F32)],
        0,
        6 * rows * chans,
        [conv_weight],
    )


def col_sets(chans):
    rest = (chans - BLOCK * LANES) // BLOCK
    return BLOCK * LANES, rest


def turn_images(ids, source, group, own):
    pixels, chans = source.shape

    def body(id_ref, i_ref, img_ref, wide):
        wide[...] = i_ref[...].astype(F32).T
        for j in range(group):
            img_ref[j] = wide[rows_at((id_ref[0] ^ j) * own, own, 8), :].astype(BF)

    return call(
        "turn_images",
        body,
        shape((group, own, pixels), BF),
        [pltpu.VMEM((chans, pixels), F32)],
        0,
        4 * pixels * chans,
        [ids, source],
        1,
    )


def back_product(ids, cots, skip_weight):
    few, wide_chans = cots[0].shape
    own = skip_weight.shape[0]
    group = len(cots)

    def body(id_ref, s_ref, *refs):
        o_ref, held = refs[group:]
        for j in range(group):
            held[rows_at((id_ref[0] ^ j) * few, few, 16), :] = refs[j][...]
        o_ref[...] = dot(s_ref[...], held[...], NT).astype(BF)

    return call(
        "back_product",
        body,
        [shape((own, group * few), BF), shape((group * few, wide_chans), BF)],
        [],
        2 * own * group * few * wide_chans,
        group * few * wide_chans * 2,
        [ids, skip_weight, *cots],
        1,
    )


def pixel_parts(pixels, width):
    at = lax.broadcasted_iota(jnp.int32, (1, pixels), 1)
    return at // width, at % width


def neighbours(value, pixels, width):
    height = pixels // width
    y, x = pixel_parts(pixels, width)
    for dy in range(3):
        for dx in range(3):
            off = (dy - 1) * width + dx - 1
            if off == 0:
                yield value
                continue
            inside = (y >= 1 - dy) & (y < height + 1 - dy) & (x >= 1 - dx) & (x < width + 1 - dx)
            yield jnp.where(inside, pltpu.roll(value, -off % pixels, 1), 0.0)


def spread_matrix(few_all, few, pixels, width):
    y, x = pixel_parts(pixels, width)
    coarse = (y // 2) * (width // 2) + x // 2
    even = (y % 2 == 0) & (x % 2 == 0)
    row = lax.broadcasted_iota(jnp.int32, (few_all, pixels), 0)
    for d in range(few_all // few):
        yield jnp.where(even & (row == d * few + coarse), 1.0, 0.0).astype(BF)


def spread_rows(few_all, few, pixels, width, d):
    at = lax.broadcasted_iota(jnp.int32, (pixels, 1), 0)
    y, x = at // width, at % width
    coarse = jnp.where((y % 2 == 0) & (x % 2 == 0), (y // 2) * (width // 2) + x // 2, -few_all)
    col = lax.broadcasted_iota(jnp.int32, (pixels, few_all), 1)
    return jnp.where(col == d * few + coarse, 1.0, 0.0).astype(BF)


def forward(ids, own_images, w_turned, width, few):
    group = len(own_images)
    own, pixels = own_images[0].shape[1:]
    chans, rows = w_turned.shape
    few_all = group * few

    def body(id_ref, w_ref, *refs):
        keep_ref, send_ref, patch, sums, moves = refs[group:]
        for m in range(group):
            v = refs[m][0].astype(F32)
            value = (v / (1.0 + jnp.exp(-v))).astype(BF).astype(F32)
            here = slice(m * pixels, (m + 1) * pixels)
            for t, moved in enumerate(neighbours(value, pixels, width)):
                patch[t * own : (t + 1) * own, here] = moved.astype(BF)
            moves[here] = spread_rows(few_all, few, pixels, width, id_ref[0] ^ m)
        out = dot(w_ref[...], patch[...])
        for m in range(group):
            piece = out[:, m * pixels : (m + 1) * pixels]
            if m % 2:
                send_ref[m // 2, :chans] = piece.astype(BF)
            else:
                keep_ref[m // 2, :chans] = piece
        evens = dot(patch[...], moves[...]).astype(BF)
        sums[...] = dot(w_ref[...], evens)
        for j in range(group):
            piece = sums[rows_at((id_ref[0] ^ j) * own, own, 8), :]
            for n in range(few_all // pixels):
                below = slice(chans + n * own, chans + (n + 1) * own)
                cols = piece[:, n * pixels : (n + 1) * pixels]
                if j % 2:
                    send_ref[j // 2, below] = cols.astype(BF)
                else:
                    keep_ref[j // 2, below] = cols

    return call(
        "forward",
        body,
        [
            shape((group // 2, chans + own * few_all // pixels, pixels), F32),
            shape((group // 2, chans + own * few_all // pixels, pixels), BF),
            shape((rows, group * pixels), BF),
        ],
        [pltpu.VMEM((chans, few_all), F32), pltpu.VMEM((group * pixels, few_all), BF)],
        2 * group * pixels * rows * (chans + few_all),
        group * chans * pixels * 3,
        [ids, w_turned, *own_images],
        1,
    )


def filter_grad(ids, patch, hidden_cots, backs, width, few, halves):
    rows = patch.shape[0]
    group = len(hidden_cots)
    pixels, chans = hidden_cots[0].shape
    own, few_all = backs[0].shape
    _, rest = col_sets(chans)
    tiles = chans // LANES
    part = round_up(-(-rows // BLOCK), 8)

    def body(id_ref, p_ref, *refs):
        cot_refs, back_refs = refs[:group], refs[group : 2 * group]
        hid = refs[2 * group]
        outs = refs[2 * group + 1 : -3]
        back, tile, last = refs[-3:]
        for j in range(group):
            back[rows_at((id_ref[0] ^ j) * own, own, 8), :] = back_refs[j][...].astype(F32)
        back_all = back[...].astype(BF)
        for j in range(group):
            d = id_ref[0] ^ j
            spread = dot(spread_rows(few_all, few, pixels, width, d), back_all, NT)
            hid[j * pixels : (j + 1) * pixels] = (cot_refs[j][...].astype(F32) + spread).astype(BF)
        total = dot(p_ref[...], hid[...])
        for n in range(tiles):
            tile[n] = total[:, n * LANES : (n + 1) * LANES]
        lane = lax.broadcasted_iota(jnp.int32, (part, LANES), 1) // rest
        for k in range(BLOCK):
            q = id_ref[1] ^ k
            share = jnp.zeros((part, LANES), F32)
            for i in range(BLOCK):
                size = min(part, rows - i * part)
                piece = tile[tiles - 1, i * part : i * part + size, :]
                if size < part:
                    piece = jnp.concatenate([piece, jnp.zeros((part - size, LANES), F32)])
                turn = ((i - q + BLOCK) % BLOCK) * rest
                share = share + jnp.where(lane == i, pltpu.roll(piece, turn, 1), 0.0)
            last[...] = share
            for h, (low, high) in enumerate(halves):
                ref = outs[2 * h + k % 2]
                main = min(high, rows)
                if low < main:
                    ref[k // 2, : main - low] = tile[q, low:main, :].astype(ref.dtype)
                if high > rows:
                    start = max(low, rows)
                    ref[k // 2, start - low :] = last[start - rows : high - rows].astype(ref.dtype)

    outs = [shape((group * pixels, chans), BF)]
    for low, high in halves:
        outs += [shape((2, high - low, LANES), F32), shape((2, high - low, LANES), BF)]
    return call(
        "filter_grad",
        body,
        outs,
        [
            pltpu.VMEM((chans, few_all), F32),
            pltpu.VMEM((tiles, rows, LANES), F32),
            pltpu.VMEM((part, LANES), F32),
        ],
        2 * group * pixels * rows * chans,
        group * pixels * chans * 4 + rows * chans * 3,
        [ids, patch, *hidden_cots, *backs],
        1,
    )


def place_grad(ids, pieces, own, chans, scale):
    rows = 9 * own
    part = round_up(-(-rows // BLOCK), 8)
    _, rest = col_sets(chans)
    tiles = chans // LANES

    def body(id_ref, *refs):
        o_ref, wide, last, sems = refs[-4:]
        lane = lax.broadcasted_iota(jnp.int32, (part, LANES), 1) // rest

        def store(where, low, piece):
            high = low + piece.shape[0]
            for t in range(9):
                lo, hi = max(low, t * own), min(high, (t + 1) * own)
                if lo < hi:
                    wide[where, pl.ds((lo - t * own) * 9 + t, hi - lo, stride=9), :] = piece[
                        lo - low : hi - low
                    ]

        def copy_out(n, where):
            at = pl.ds(pl.multiple_of(where * LANES, LANES), LANES)
            return pltpu.make_async_copy(wide.at[where], o_ref.at[:, at], sems.at[n])

        last[...] = jnp.zeros_like(last)
        for k in range(BLOCK):
            q = id_ref[1] ^ k
            for n, (low, high, members, _) in enumerate(pieces):
                if k not in members:
                    continue
                at, main = members.index(k), min(high, rows)
                if low < main:
                    store(q, low, refs[n][at, : main - low, :].astype(F32) * scale)
                if high > rows:
                    assert low <= rows and high >= rows + part
                    share = refs[n][at, rows - low : rows - low + part, :].astype(F32) * scale
                    for i in range(BLOCK):
                        turn = ((q - i + BLOCK) % BLOCK) * rest
                        last[i] += jnp.where(lane == q, pltpu.roll(share, turn, 1), 0.0)
            copy_out(k, q).start()
        for i in range(BLOCK):
            store(BLOCK, i * part, last[i, : min(part, rows - i * part), :])
        copy_out(BLOCK, BLOCK).start()
        for k in range(BLOCK):
            copy_out(k, id_ref[1] ^ k).wait()
        copy_out(BLOCK, BLOCK).wait()

    return pl.pallas_call(
        body,
        out_shape=shape((rows, chans), F32),
        in_specs=[pl.BlockSpec(memory_space=pltpu.SMEM)]
        + [pl.BlockSpec(memory_space=pltpu.VMEM)] * len(pieces),
        out_specs=pl.BlockSpec(memory_space=pl.ANY),
        scratch_shapes=[
            pltpu.VMEM((tiles, rows, LANES), F32),
            pltpu.VMEM((BLOCK, part, LANES), F32),
            pltpu.SemaphoreType.DMA((BLOCK + 1,)),
        ],
        compiler_params=pltpu.CompilerParams(vmem_limit_bytes=VMEM_LIMIT),
        cost_estimate=pl.CostEstimate(
            flops=0, bytes_accessed=rows * chans * 6, transcendentals=0
        ),
        name="place_grad",
    )(ids, *[array for *_, array in pieces])


def finish_hidden(source, held, got, width):
    pixels, chans = source.shape
    few = pixels // 4

    def body(s_ref, k_ref, g_ref, o_ref, sub_ref):
        total = (k_ref[0, :chans] + g_ref[0, :chans].astype(F32)).T
        hidden = (s_ref[...].astype(F32) + total).astype(BF)
        o_ref[...] = hidden
        (one_hot,) = spread_matrix(few, few, pixels, width)
        sub_ref[...] = dot(one_hot, hidden).astype(BF)

    return call(
        "finish_hidden",
        body,
        [shape((pixels, chans), BF), shape((few, chans), BF)],
        [],
        2 * few * pixels * chans,
        pixels * chans * 10,
        [source, held, got],
    )


def skip_grad_term(ids, held, got, own_images, cots, width, few):
    group = len(own_images)
    own, pixels = own_images[0].shape[1:]
    few_all, wide_chans = cots.shape
    blocks = few_all // pixels
    low = held.shape[1] - own * blocks
    part, tiles = own // BLOCK, wide_chans // LANES

    def body(id_ref, k_ref, g_ref, c_ref, *refs):
        keep_ref, send_ref, total = refs[-3:]
        sub = k_ref[0, low:] + g_ref[0, low:].astype(F32)
        sub = jnp.concatenate([sub[n * own : (n + 1) * own] for n in range(blocks)], axis=1)
        row = lax.broadcasted_iota(jnp.int32, (few_all, pixels), 0) // few
        every = jnp.zeros((few_all, pixels), F32)
        for matrix in spread_matrix(few_all, few, pixels, width):
            every = every + matrix.astype(F32)
        for j in range(group):
            chosen = jnp.where(row == (id_ref[0] ^ j), every, 0.0).astype(BF)
            sub = sub + dot(refs[j][0], chosen, NT)
        total[...] = dot(sub.astype(BF), c_ref[...])
        for k in range(BLOCK):
            piece = total[rows_at((id_ref[1] ^ k) * part, part, 8), :]
            ref = send_ref if k % 2 else keep_ref
            for n in range(tiles):
                cols = piece[:, n * LANES : (n + 1) * LANES]
                ref[k // 2, n * part : (n + 1) * part] = cols.astype(ref.dtype)

    return call(
        "skip_grad_term",
        body,
        [shape((2, part * tiles, LANES), F32), shape((2, part * tiles, LANES), BF)],
        [pltpu.VMEM((own, wide_chans), F32)],
        2 * own * few_all * wide_chans,
        own * wide_chans * 4,
        [ids, held, got, cots, *own_images],
        1,
    )


def project(ids, sub, skips):
    few, chans = sub.shape
    own, wide_chans = skips[0].shape
    group = len(skips)

    def body(id_ref, s_ref, *refs):
        o_ref, turned = refs[group:]
        turned[...] = s_ref[...].astype(F32).T
        total = jnp.zeros((few, wide_chans), F32)
        for j in range(group):
            rows = turned[rows_at((id_ref[0] ^ j) * own, own, 8), :].astype(BF)
            total = total + dot(rows, refs[j][...], TN)
        o_ref[...] = total.astype(BF)

    return call(
        "project",
        body,
        shape((few, wide_chans), BF),
        [pltpu.VMEM((chans, few), F32)],
        2 * few * chans * wide_chans,
        chans * wide_chans * 2,
        [ids, sub, *skips],
        1,
    )


def image_grad(ids, hidden_grad, own_images, w_tap, width):
    group = len(own_images)
    own, pixels = own_images[0].shape[1:]
    rows, chans = w_tap.shape
    height = pixels // width

    def body(id_ref, h_ref, w_ref, *refs):
        img_refs = refs[:group]
        o_ref, turned, tap = refs[group:]
        y, x = pixel_parts(pixels, width)
        for j in range(group):
            hid = h_ref[j * pixels : (j + 1) * pixels]
            turned[...] = hid.astype(F32).T
            tap[...] = dot(w_ref[...], hid, NT)
            side = tap[4 * own : 5 * own]
            for dy in range(3):
                for dx in range(3):
                    off = (dy - 1) * width + dx - 1
                    if off == 0:
                        continue
                    inside = (y >= dy - 1) & (y < height + dy - 1)
                    inside = inside & (x >= dx - 1) & (x < width + dx - 1)
                    t = 3 * dy + dx
                    moved = pltpu.roll(tap[t * own : (t + 1) * own], off % pixels, 1)
                    side = side + jnp.where(inside, moved, 0.0)
            v = img_refs[j][0].astype(F32)
            sig = 1.0 / (1.0 + jnp.exp(-v))
            slope = sig * (1.0 + v * (1.0 - sig))
            mine = turned[rows_at(id_ref[0] * own, own, 8), :]
            o_ref[j] = (mine + slope * side).astype(BF)

    return call(
        "image_grad",
        body,
        shape((group, own, pixels), BF),
        [pltpu.VMEM((chans, pixels), F32), pltpu.VMEM((rows, pixels), F32)],
        2 * group * pixels * rows * chans,
        group * pixels * chans * 2,
        [ids, hidden_grad, w_tap, *own_images],
        1,
    )


def finish_images(ids, pieces, chans):
    group = len(pieces)
    own, pixels = pieces[0].shape[1:]

    def body(id_ref, *refs):
        o_ref, wide = refs[group:]
        for j in range(group):
            wide[rows_at((id_ref[0] ^ j) * own, own, 8), :] = refs[j][0].astype(F32)
        o_ref[...] = wide[...].T.astype(BF)

    return call(
        "finish_images",
        body,
        shape((pixels, chans), BF),
        [pltpu.VMEM((chans, pixels), F32)],
        0,
        pixels * chans * 4,
        [ids, *pieces],
        1,
    )


def flip(value, axis, bit):
    return lax.ppermute(value, axis, [(i, i ^ bit) for i in range(lax.axis_size(axis))])


def after(value, *others):
    return lax.optimization_barrier((value, *others))[0]


def high_bits(count):
    return [1 << k for k in reversed(range(count.bit_length() - 1))]


def gather(value, axis, *others):
    found = {0: value}
    for n, bit in enumerate(high_bits(lax.axis_size(axis))):
        for j, held in list(found.items()):
            if n == 1 and j and others:
                held = found[j] = after(held, *others)
            found[j ^ bit] = flip(held, axis, bit)
    return [found[j] for j in range(len(found))]


def exchange(blocks, axis, count):
    return [flip(blocks[j : j + 1], axis, j) if j else blocks[:1] for j in range(count)]


def hop(value, bit):
    ranks, group = lax.axis_size("rep"), lax.axis_size("shard")
    pairs = []
    for r in range(ranks):
        for s in range(group):
            other = r ^ (bit if s % 2 == 0 else 3 - bit)
            pairs.append((r * group + s, other * group + s))
    return lax.ppermute(value, ("rep", "shard"), pairs)


def block_gather(value):
    pair = jnp.stack([value, hop(value, 2)])
    return [((0, 2), pair), ((1, 3), hop(pair, 1))]


def add_beyond_block(value):
    for bit in reversed(high_bits(lax.axis_size("rep"))):
        if bit >= BLOCK:
            got = flip(value, "rep", bit)
            value = (value.astype(F32) + got.astype(F32)).astype(BF)
    return value


def sum_scatter(keep, send):
    bits = list(reversed(high_bits(lax.axis_size("shard"))))
    for bit in bits[:-1]:
        total = keep + flip(send, "shard", bit).astype(F32)
        keep, send = total[0::2], total[1::2].astype(BF)
    return keep, flip(send, "shard", bits[-1])


def on_device(images, conv_weight, skip_weight, cotangent, hidden_cot):
    _, height, width, chans = images.shape
    own, wide = skip_weight.shape
    pixels, few = height * width, (height // 2) * (width // 2)
    group, ranks = lax.axis_size("shard"), lax.axis_size("rep")
    shard, rank = lax.axis_index("shard"), lax.axis_index("rep") % BLOCK
    member = jnp.where(shard % 2 == 0, rank, rank // 2 + 2 * (rank % 2))
    ids = jnp.stack([shard, member]).astype(jnp.int32)
    source = images.reshape(pixels, chans)

    img_sets = turn_images(ids, source, group, own)
    cots = gather(cotangent.reshape(few, wide), "shard", img_sets)
    own_images = exchange(img_sets, "shard", group)
    hidden_cots = gather(after(hidden_cot.reshape(pixels, chans), img_sets), "shard")
    back, cots = back_product(ids, cots, skip_weight)
    backs = [back] + [flip(back, "shard", j) for j in range(1, group)]
    w_tap, w_turned = turn_filters(after(conv_weight, back, *own_images))

    keep, send, patch = forward(after(ids, *backs, hidden_cots[2]), own_images, w_turned, width, few)

    rows = 9 * own
    part = round_up(-(-rows // BLOCK), 8)
    cut = min(round_up((rows + part) // 2, 8), rows)
    halves = [(0, cut), (cut, rows + part)]
    hidden_grad, keep_a, send_a, keep_b, send_b = filter_grad(
        ids, patch, hidden_cots, backs, width, few, halves
    )
    got_a, got_b = hop(send_a, 1), hop(send_b, 1)
    keep, got = sum_scatter(keep, send)
    own_input = image_grad(ids, hidden_grad, own_images, w_tap, width)
    got_a, own_input = lax.optimization_barrier((got_a, own_input))
    mid_a = (keep_a[1] + got_a[1].astype(F32)).astype(BF)
    last_a = hop(mid_a, 2)
    got_b = after(got_b, mid_a)
    mid_b = (keep_b[1] + got_b[1].astype(F32)).astype(BF)
    last_b = hop(mid_b, 2)
    sum_a = (keep_a[0] + got_a[0].astype(F32) + last_a.astype(F32)).astype(BF)
    full_a = add_beyond_block(sum_a)
    last_b = after(last_b, sum_a)
    sum_b = (keep_b[0] + got_b[0].astype(F32) + last_b.astype(F32)).astype(BF)
    full_b = add_beyond_block(sum_b)

    skip_keep, skip_send = skip_grad_term(
        after(ids, sum_b), keep, got, own_images, cots, width, few
    )
    got_s = hop(skip_send, 1)
    hidden, sub = finish_hidden(after(source, skip_send), keep, got, width)
    got_s, hidden = lax.optimization_barrier((got_s, hidden))
    mid_s = (skip_keep[1] + got_s[1].astype(F32)).astype(BF)
    last_s = hop(mid_s, 2)
    arrived = exchange(after(own_input, mid_b), "shard", group)
    input_grad = finish_images(after(ids, mid_s), arrived, chans)
    last_s, input_grad = lax.optimization_barrier((last_s, input_grad))
    sum_s = (skip_keep[0] + got_s[0].astype(F32) + last_s.astype(F32)).astype(BF)
    full_s = add_beyond_block(sum_s)
    skips = gather(after(skip_weight, mid_b), "shard")
    projected = project(after(ids, sum_s), sub, skips).reshape(cotangent.shape)
    sum_a, sum_b, sum_s = full_a, full_b, full_s
    sum_a = block_gather(sum_a)
    sum_b = block_gather(jnp.concatenate([sum_b, sum_s]))
    factor = 1.0 / math.sqrt(ranks * group * few)
    pieces = [(*halves[0], *pair) for pair in sum_a] + [(*halves[1], *pair) for pair in sum_b]
    conv_grad = place_grad(ids, pieces, own, chans, factor)
    skip_sum = {}
    for members, array in sum_b:
        for n, k in enumerate(members):
            skip_sum[k] = array[n, -sum_s.shape[0] :]
    skip_sum = jnp.stack([skip_sum[k] for k in range(BLOCK)])
    skip_sum = skip_sum[jnp.arange(BLOCK, dtype=jnp.int32) ^ member].astype(F32) * factor
    skip_sum = skip_sum.reshape(BLOCK, wide // LANES, own // BLOCK, LANES)
    skip_grad = skip_sum.transpose(0, 2, 1, 3).reshape(own, wide)

    return (
        hidden.reshape(images.shape),
        projected,
        input_grad.reshape(images.shape),
        conv_grad,
        skip_grad,
    )


def solution(mesh):
    placed = (
        P(("rep", "shard"), None, None, None),
        P("shard", None),
        P("shard", None),
        P(("rep", "shard"), None, None, None),
        P(("rep", "shard"), None, None, None),
    )
    return jax.shard_map(
        on_device,
        mesh=mesh,
        in_specs=placed,
        out_specs=(
            P(("rep", "shard"), None, None, None),
            P(("rep", "shard"), None, None, None),
            P(("rep", "shard"), None, None, None),
            P("shard", None),
            P("shard", None),
        ),
        check_vma=False,
    )
```

```python
import math

import jax
import jax.numpy as jnp
from jax import lax
from jax.experimental import pallas as pl
from jax.experimental.pallas import tpu as pltpu
from jax.sharding import PartitionSpec as P

BF = jnp.bfloat16
F32 = jnp.float32
VMEM_LIMIT = 56 << 20
LANES = 128
BLOCK = 4


def dot(a, b, dims=((1,), (0,))):
    return lax.dot_general(a, b, (dims, ((), ())), preferred_element_type=F32)


NT = ((1,), (1,))
TN = ((0,), (0,))


def call(name, body, outs, scratch, flops, moved, args, scalars=0):
    specs = [
        pl.BlockSpec(memory_space=pltpu.SMEM if i < scalars else pltpu.VMEM)
        for i in range(len(args))
    ]
    return pl.pallas_call(
        body,
        out_shape=outs,
        in_specs=specs,
        out_specs=jax.tree.map(lambda _: pl.BlockSpec(memory_space=pltpu.VMEM), outs),
        scratch_shapes=scratch,
        compiler_params=pltpu.CompilerParams(vmem_limit_bytes=VMEM_LIMIT),
        cost_estimate=pl.CostEstimate(flops=flops, bytes_accessed=moved, transcendentals=0),
        name=name,
    )(*args)


def shape(dims, kind):
    return jax.ShapeDtypeStruct(dims, kind)


def rows_at(start, size, step):
    return pl.ds(pl.multiple_of(start, step), size)


def round_up(value, step):
    return -(-value // step) * step


def turn_filters(conv_weight):
    rows, chans = conv_weight.shape
    own = rows // 9

    def body(w_ref, o_ref, t_ref, wide):
        for k in range(chans // LANES):
            cols = slice(k * LANES, (k + 1) * LANES)
            wide[k] = w_ref[:, cols].astype(F32)
            for t in range(9):
                piece = wide[k, pl.ds(t, own, stride=9), :]
                o_ref[t * own : (t + 1) * own, cols] = piece.astype(BF)
        t_ref[...] = o_ref[...].T

    return call(
        "turn_filters",
        body,
        [shape((rows, chans), BF), shape((chans, rows), BF)],
        [pltpu.VMEM((chans // LANES, rows, LANES), F32)],
        0,
        6 * rows * chans,
        [conv_weight],
    )


def col_sets(chans):
    rest = (chans - BLOCK * LANES) // BLOCK
    return BLOCK * LANES, rest


def turn_images(ids, source, group, own):
    pixels, chans = source.shape

    def body(id_ref, i_ref, *refs):
        wide = refs[group]
        wide[...] = i_ref[...].astype(F32).T
        for j in range(group):
            refs[j][...] = wide[rows_at((id_ref[0] ^ j) * own, own, 8), :].astype(BF)

    return call(
        "turn_images",
        body,
        [shape((own, pixels), BF)] * group,
        [pltpu.VMEM((chans, pixels), F32)],
        0,
        4 * pixels * chans,
        [ids, source],
        1,
    )


def back_product(ids, cots, skip_weight):
    few, wide_chans = cots[0].shape
    own = skip_weight.shape[0]
    group = len(cots)

    def body(id_ref, s_ref, *refs):
        o_ref, held = refs[group:]
        for j in range(group):
            held[rows_at((id_ref[0] ^ j) * few, few, 16), :] = refs[j][...]
        o_ref[...] = dot(s_ref[...], held[...], NT).astype(BF)

    return call(
        "back_product",
        body,
        [shape((own, group * few), BF), shape((group * few, wide_chans), BF)],
        [],
        2 * own * group * few * wide_chans,
        group * few * wide_chans * 2,
        [ids, skip_weight, *cots],
        1,
    )


def pixel_parts(pixels, width):
    at = lax.broadcasted_iota(jnp.int32, (1, pixels), 1)
    return at // width, at % width


def neighbours(value, pixels, width):
    height = pixels // width
    y, x = pixel_parts(pixels, width)
    for dy in range(3):
        for dx in range(3):
            off = (dy - 1) * width + dx - 1
            if off == 0:
                yield value
                continue
            inside = (y >= 1 - dy) & (y < height + 1 - dy) & (x >= 1 - dx) & (x < width + 1 - dx)
            yield jnp.where(inside, pltpu.roll(value, -off % pixels, 1), 0.0)


def spread_matrix(few_all, few, pixels, width):
    y, x = pixel_parts(pixels, width)
    coarse = (y // 2) * (width // 2) + x // 2
    even = (y % 2 == 0) & (x % 2 == 0)
    row = lax.broadcasted_iota(jnp.int32, (few_all, pixels), 0)
    for d in range(few_all // few):
        yield jnp.where(even & (row == d * few + coarse), 1.0, 0.0).astype(BF)


def spread_rows(few_all, few, pixels, width, d):
    at = lax.broadcasted_iota(jnp.int32, (pixels, 1), 0)
    y, x = at // width, at % width
    coarse = jnp.where((y % 2 == 0) & (x % 2 == 0), (y // 2) * (width // 2) + x // 2, -few_all)
    col = lax.broadcasted_iota(jnp.int32, (pixels, few_all), 1)
    return jnp.where(col == d * few + coarse, 1.0, 0.0).astype(BF)


def make_patches(own_images, width):
    group = len(own_images)
    own, pixels = own_images[0].shape

    def body(*refs):
        patch = refs[group]
        for m in range(group):
            v = refs[m][...].astype(F32)
            value = (v / (1.0 + jnp.exp(-v))).astype(BF).astype(F32)
            here = slice(m * pixels, (m + 1) * pixels)
            for t, moved in enumerate(neighbours(value, pixels, width)):
                patch[t * own : (t + 1) * own, here] = moved.astype(BF)

    return call(
        "make_patches",
        body,
        shape((9 * own, group * pixels), BF),
        [],
        0,
        20 * own * group * pixels,
        own_images,
    )


def forward(ids, patch, w_turned, pixels, width, few):
    chans, rows = w_turned.shape
    group, own = patch.shape[1] // pixels, rows // 9
    few_all = group * few

    def body(id_ref, w_ref, p_ref, *refs):
        keep_refs = refs[: group // 2]
        send_ref, sums, moves = refs[group // 2 :]
        for m in range(group):
            here = slice(m * pixels, (m + 1) * pixels)
            moves[here] = spread_rows(few_all, few, pixels, width, id_ref[0] ^ m)
        out = dot(w_ref[...], p_ref[...])
        for m in range(group):
            piece = out[:, m * pixels : (m + 1) * pixels]
            if m % 2:
                send_ref[m // 2, :chans] = piece.astype(BF)
            else:
                keep_refs[m // 2][:chans] = piece
        evens = dot(p_ref[...], moves[...]).astype(BF)
        sums[...] = dot(w_ref[...], evens)
        for j in range(group):
            piece = sums[rows_at((id_ref[0] ^ j) * own, own, 8), :]
            for n in range(few_all // pixels):
                below = slice(chans + n * own, chans + (n + 1) * own)
                cols = piece[:, n * pixels : (n + 1) * pixels]
                if j % 2:
                    send_ref[j // 2, below] = cols.astype(BF)
                else:
                    keep_refs[j // 2][below] = cols

    return call(
        "forward",
        body,
        [shape((chans + own * few_all // pixels, pixels), F32)] * (group // 2)
        + [shape((group // 2, chans + own * few_all // pixels, pixels), BF)],
        [pltpu.VMEM((chans, few_all), F32), pltpu.VMEM((group * pixels, few_all), BF)],
        2 * group * pixels * rows * (chans + few_all),
        group * chans * pixels * 3,
        [ids, w_turned, patch],
        1,
    )


def filter_grad(ids, patch, hidden_cots, backs, width, few):
    rows = patch.shape[0]
    group = len(hidden_cots)
    pixels, chans = hidden_cots[0].shape
    own, few_all = backs[0].shape
    _, rest = col_sets(chans)
    tiles = chans // LANES
    part = round_up(-(-rows // BLOCK), 8)

    def body(id_ref, p_ref, *refs):
        cot_refs, back_refs = refs[:group], refs[group : 2 * group]
        hid = refs[2 * group]
        keep_refs, send_ref = refs[-5:-3], refs[-3]
        back, tile = refs[-2:]
        for j in range(group):
            back[rows_at((id_ref[0] ^ j) * own, own, 8), :] = back_refs[j][...].astype(F32)
        back_all = back[...].astype(BF)
        for j in range(group):
            d = id_ref[0] ^ j
            spread = dot(spread_rows(few_all, few, pixels, width, d), back_all, NT)
            hid[j * pixels : (j + 1) * pixels] = (cot_refs[j][...].astype(F32) + spread).astype(BF)
        total = dot(p_ref[...], hid[...])
        for n in range(tiles):
            tile[n] = total[:, n * LANES : (n + 1) * LANES]
        lane = lax.broadcasted_iota(jnp.int32, (part, LANES), 1) // rest
        for k in (1, 3, 0, 2):
            q = id_ref[1] ^ k
            share = jnp.zeros((part, LANES), F32)
            for i in range(BLOCK):
                size = min(part, rows - i * part)
                piece = tile[tiles - 1, i * part : i * part + size, :]
                if size < part:
                    piece = jnp.concatenate([piece, jnp.zeros((part - size, LANES), F32)])
                turn = ((i - q + BLOCK) % BLOCK) * rest
                share = share + jnp.where(lane == i, pltpu.roll(piece, turn, 1), 0.0)
            if k % 2:
                send_ref[k // 2, :rows] = tile[q].astype(BF)
                send_ref[k // 2, rows:] = share.astype(BF)
            else:
                keep_refs[k // 2][:rows] = tile[q]
                keep_refs[k // 2][rows:] = share

    return call(
        "filter_grad",
        body,
        [
            shape((group * pixels, chans), BF),
            shape((rows + part, LANES), F32),
            shape((rows + part, LANES), F32),
            shape((2, rows + part, LANES), BF),
        ],
        [
            pltpu.VMEM((chans, few_all), F32),
            pltpu.VMEM((tiles, rows, LANES), F32),
        ],
        2 * group * pixels * rows * chans,
        group * pixels * chans * 4 + rows * chans * 3,
        [ids, patch, *hidden_cots, *backs],
        1,
    )


def place_grad(ids, members, array, own, chans, scale, begun=None):
    rows = 9 * own
    part = round_up(-(-rows // BLOCK), 8)
    _, rest = col_sets(chans)
    tiles = chans // LANES
    final = begun is not None

    def body(id_ref, p_ref, *refs):
        if final:
            _, begun_ref, o_ref, wide, last, sems = refs
            last[...] = begun_ref[...]
        else:
            o_ref, last, wide, sems = refs
            last[...] = jnp.zeros_like(last)
        lane = lax.broadcasted_iota(jnp.int32, (part, LANES), 1) // rest

        def store(where, low, piece):
            high = low + piece.shape[0]
            for t in range(9):
                lo, hi = max(low, t * own), min(high, (t + 1) * own)
                if lo < hi:
                    wide[where, pl.ds((lo - t * own) * 9 + t, hi - lo, stride=9), :] = piece[
                        lo - low : hi - low
                    ]

        def copy_out(slot, where):
            at = pl.ds(pl.multiple_of(where * LANES, LANES), LANES)
            return pltpu.make_async_copy(wide.at[slot], o_ref.at[:, at], sems.at[slot])

        for n, k in enumerate(members):
            q = id_ref[1] ^ k
            store(n, 0, p_ref[n, :rows, :].astype(F32) * scale)
            copy_out(n, q).start()
            share = p_ref[n, rows:, :].astype(F32) * scale
            for i in range(BLOCK):
                turn = ((q - i + BLOCK) % BLOCK) * rest
                last[i] += jnp.where(lane == q, pltpu.roll(share, turn, 1), 0.0)
        if final:
            for i in range(BLOCK):
                store(2, i * part, last[i, : min(part, rows - i * part), :])
            copy_out(2, tiles - 1).start()
        for n, k in enumerate(members):
            copy_out(n, id_ref[1] ^ k).wait()
        if final:
            copy_out(2, tiles - 1).wait()

    vmem, anywhere = pl.BlockSpec(memory_space=pltpu.VMEM), pl.BlockSpec(memory_space=pl.ANY)
    share_shape = (BLOCK, part, LANES)
    scratch = [pltpu.VMEM((3, rows, LANES), F32)]
    if final:
        scratch.append(pltpu.VMEM(share_shape, F32))
    return pl.pallas_call(
        body,
        out_shape=shape((rows, chans), F32)
        if final
        else [shape((rows, chans), F32), shape(share_shape, F32)],
        in_specs=[pl.BlockSpec(memory_space=pltpu.SMEM), vmem] + [anywhere, vmem] * final,
        out_specs=anywhere if final else [anywhere, vmem],
        scratch_shapes=scratch + [pltpu.SemaphoreType.DMA((3,))],
        input_output_aliases={2: 0} if final else {},
        compiler_params=pltpu.CompilerParams(vmem_limit_bytes=VMEM_LIMIT),
        cost_estimate=pl.CostEstimate(
            flops=0, bytes_accessed=rows * chans * 3, transcendentals=0
        ),
        name="place_grad",
    )(ids, array, *(begun or ()))


def place_skip(ids, pieces, own, wide_chans, scale):
    few_rows = own // BLOCK

    def body(id_ref, *refs):
        o_ref, shares = refs[-2:]
        for ref, (members, _) in zip(refs, pieces):
            for n, k in enumerate(members):
                for i in range(wide_chans // LANES):
                    piece = ref[n, i * few_rows : (i + 1) * few_rows, :].astype(F32) * scale
                    shares[id_ref[1] ^ k, :, i * LANES : (i + 1) * LANES] = piece
        for q in range(BLOCK):
            o_ref[q * few_rows : (q + 1) * few_rows] = shares[q]

    return call(
        "place_skip",
        body,
        shape((own, wide_chans), F32),
        [pltpu.VMEM((BLOCK, few_rows, wide_chans), F32)],
        0,
        6 * own * wide_chans,
        [ids, *[array for _, array in pieces]],
        1,
    )


def finish_hidden(source, held, got, width):
    pixels, chans = source.shape
    few = pixels // 4

    def body(s_ref, k_ref, g_ref, o_ref, sub_ref):
        total = (k_ref[:chans] + g_ref[:chans].astype(F32)).T
        hidden = (s_ref[...].astype(F32) + total).astype(BF)
        o_ref[...] = hidden
        (one_hot,) = spread_matrix(few, few, pixels, width)
        sub_ref[...] = dot(one_hot, hidden).astype(BF)

    return call(
        "finish_hidden",
        body,
        [shape((pixels, chans), BF), shape((few, chans), BF)],
        [],
        2 * few * pixels * chans,
        pixels * chans * 10,
        [source, held, got],
    )


def skip_grad_term(ids, held, got, own_images, cots, width, few):
    group = len(own_images)
    own, pixels = own_images[0].shape
    few_all, wide_chans = cots.shape
    blocks = few_all // pixels
    low = held.shape[0] - own * blocks
    part, tiles = own // BLOCK, wide_chans // LANES

    def body(id_ref, k_ref, g_ref, c_ref, *refs):
        keep_refs, send_ref, total = refs[-4:-2], refs[-2], refs[-1]
        sub = k_ref[low:] + g_ref[low:].astype(F32)
        sub = jnp.concatenate([sub[n * own : (n + 1) * own] for n in range(blocks)], axis=1)
        row = lax.broadcasted_iota(jnp.int32, (few_all, pixels), 0) // few
        every = jnp.zeros((few_all, pixels), F32)
        for matrix in spread_matrix(few_all, few, pixels, width):
            every = every + matrix.astype(F32)
        for j in range(group):
            chosen = jnp.where(row == (id_ref[0] ^ j), every, 0.0).astype(BF)
            sub = sub + dot(refs[j][...], chosen, NT)
        term = dot(sub.astype(BF), c_ref[...])
        for q in range(BLOCK):
            total[q] = term[q * part : (q + 1) * part]
        for k in range(BLOCK):
            piece = total[id_ref[1] ^ k]
            ref = send_ref.at[k // 2] if k % 2 else keep_refs[k // 2]
            for n in range(tiles):
                cols = piece[:, n * LANES : (n + 1) * LANES]
                ref[n * part : (n + 1) * part] = cols.astype(ref.dtype)

    return call(
        "skip_grad_term",
        body,
        [shape((part * tiles, LANES), F32)] * 2 + [shape((2, part * tiles, LANES), BF)],
        [pltpu.VMEM((BLOCK, part, wide_chans), F32)],
        2 * own * few_all * wide_chans,
        own * wide_chans * 4,
        [ids, held, got, cots, *own_images],
        1,
    )


def project(ids, sub, skips):
    few, chans = sub.shape
    own, wide_chans = skips[0].shape
    group = len(skips)

    def body(id_ref, s_ref, *refs):
        o_ref, turned = refs[group:]
        turned[...] = s_ref[...].astype(F32).T
        total = jnp.zeros((few, wide_chans), F32)
        for j in range(group):
            rows = turned[rows_at((id_ref[0] ^ j) * own, own, 8), :].astype(BF)
            total = total + dot(rows, refs[j][...], TN)
        o_ref[...] = total.astype(BF)

    return call(
        "project",
        body,
        shape((few, wide_chans), BF),
        [pltpu.VMEM((chans, few), F32)],
        2 * few * chans * wide_chans,
        chans * wide_chans * 2,
        [ids, sub, *skips],
        1,
    )


def image_grad(ids, hidden_grad, own_images, w_tap, width):
    group = len(own_images)
    own, pixels = own_images[0].shape
    rows, chans = w_tap.shape
    height = pixels // width

    def body(id_ref, h_ref, w_ref, *refs):
        img_refs = refs[:group]
        o_refs, turned, tap = refs[group:-2], refs[-2], refs[-1]
        y, x = pixel_parts(pixels, width)
        for j in range(group):
            hid = h_ref[j * pixels : (j + 1) * pixels]
            turned[...] = hid.astype(F32).T
            tap[...] = dot(w_ref[...], hid, NT)
            side = tap[4 * own : 5 * own]
            for dy in range(3):
                for dx in range(3):
                    off = (dy - 1) * width + dx - 1
                    if off == 0:
                        continue
                    inside = (y >= dy - 1) & (y < height + dy - 1)
                    inside = inside & (x >= dx - 1) & (x < width + dx - 1)
                    t = 3 * dy + dx
                    moved = pltpu.roll(tap[t * own : (t + 1) * own], off % pixels, 1)
                    side = side + jnp.where(inside, moved, 0.0)
            v = img_refs[j][...].astype(F32)
            sig = 1.0 / (1.0 + jnp.exp(-v))
            slope = sig * (1.0 + v * (1.0 - sig))
            mine = turned[rows_at(id_ref[0] * own, own, 8), :]
            o_refs[j][...] = (mine + slope * side).astype(BF)

    return call(
        "image_grad",
        body,
        [shape((own, pixels), BF)] * group,
        [pltpu.VMEM((chans, pixels), F32), pltpu.VMEM((rows, pixels), F32)],
        2 * group * pixels * rows * chans,
        group * pixels * chans * 2,
        [ids, hidden_grad, w_tap, *own_images],
        1,
    )


def finish_images(ids, pieces, chans):
    group = len(pieces)
    own, pixels = pieces[0].shape

    def body(id_ref, *refs):
        o_ref, wide = refs[group:]
        for j in range(group):
            wide[rows_at((id_ref[0] ^ j) * own, own, 8), :] = refs[j][...].astype(F32)
        o_ref[...] = wide[...].T.astype(BF)

    return call(
        "finish_images",
        body,
        shape((pixels, chans), BF),
        [pltpu.VMEM((chans, pixels), F32)],
        0,
        pixels * chans * 4,
        [ids, *pieces],
        1,
    )


def flip(value, axis, bit):
    return lax.ppermute(value, axis, [(i, i ^ bit) for i in range(lax.axis_size(axis))])


def after(value, *others):
    return lax.optimization_barrier((value, *others))[0]


def high_bits(count):
    return [1 << k for k in reversed(range(count.bit_length() - 1))]


def gather(value, axis, *others):
    found = {0: value}
    for n, bit in enumerate(high_bits(lax.axis_size(axis))):
        for j, held in list(found.items()):
            if n == 1 and j and others:
                held = found[j] = after(held, *others)
            found[j ^ bit] = flip(held, axis, bit)
    return [found[j] for j in range(len(found))]


def exchange(blocks, axis, count):
    return [flip(blocks[j], axis, j) if j else blocks[0] for j in range(count)]


def hop(value, bit):
    ranks, group = lax.axis_size("rep"), lax.axis_size("shard")
    pairs = []
    for r in range(ranks):
        for s in range(group):
            other = r ^ (bit if s % 2 == 0 else 3 - bit)
            pairs.append((r * group + s, other * group + s))
    return lax.ppermute(value, ("rep", "shard"), pairs)


def sum_beyond_block(value):
    bits = [bit for bit in reversed(high_bits(lax.axis_size("rep"))) if bit >= BLOCK]
    got = jnp.zeros_like(value)
    for n, bit in enumerate(bits):
        if n:
            value = (value.astype(F32) + got.astype(F32)).astype(BF)
        got = flip(value, "rep", bit)
    return value, got


def add_beyond_block(value):
    value, got = sum_beyond_block(value)
    return (value.astype(F32) + got.astype(F32)).astype(BF)


def sum_scatter(keep, send):
    bits = list(reversed(high_bits(lax.axis_size("shard"))))
    for bit in bits[:-1]:
        got = flip(send, "shard", bit)
        total = [held + got[i].astype(F32) for i, held in enumerate(keep)]
        keep, send = total[0::2], jnp.stack(total[1::2]).astype(BF)
    return keep[0], send[0], flip(send[0], "shard", bits[-1])


def on_device(images, conv_weight, skip_weight, cotangent, hidden_cot):
    _, height, width, chans = images.shape
    own, wide = skip_weight.shape
    pixels, few = height * width, (height // 2) * (width // 2)
    group, ranks = lax.axis_size("shard"), lax.axis_size("rep")
    shard, rank = lax.axis_index("shard"), lax.axis_index("rep") % BLOCK
    member = jnp.where(shard % 2 == 0, rank, rank // 2 + 2 * (rank % 2))
    ids = jnp.stack([shard, member]).astype(jnp.int32)
    source = images.reshape(pixels, chans)

    img_sets = turn_images(ids, source, group, own)
    cots = gather(cotangent.reshape(few, wide), "shard", img_sets[0])
    own_images = exchange(img_sets, "shard", group)
    back, cots = back_product(after(ids, *own_images), cots, skip_weight)
    backs = [back] + [flip(back, "shard", j) for j in range(1, group)]
    patch = make_patches([after(piece, back) for piece in own_images], width)
    hidden_cots = hidden_cot.reshape(pixels, chans)
    hidden_cots = gather(after(hidden_cots, *own_images[2:]), "shard", patch, *backs)

    hidden_grad, keep_0, keep_2, send_g = filter_grad(
        after(ids, patch), patch, hidden_cots, backs, width, few
    )
    got_g = hop(send_g, 1)
    w_tap, w_turned = turn_filters(after(conv_weight, send_g))
    *keep, send = forward(ids, patch, w_turned, pixels, width, few)
    skips = gather(after(skip_weight, send_g), "shard")
    got_g = after(got_g, send, skips[2])
    mid_g = (keep_2 + got_g[1].astype(F32)).astype(BF)
    last_g = hop(mid_g, 2)
    keep, last, got = sum_scatter(keep, after(send, mid_g))
    own_input = image_grad(after(ids, last), hidden_grad, own_images, w_tap, width)
    last_g = after(last_g, own_input[0], got, *skips)
    sum_g = (keep_0 + got_g[0].astype(F32) + last_g.astype(F32)).astype(BF)

    beyond = sum_beyond_block(sum_g)
    skip_0, skip_2, send_s = skip_grad_term(
        after(ids, sum_g), keep, got, own_images, cots, width, few
    )
    hidden, sub = finish_hidden(after(source, sum_g), keep, got, width)
    got_s = hop(send_s, 1)
    projected = project(ids, sub, skips).reshape(cotangent.shape)
    got_s, far, projected = lax.optimization_barrier((got_s, beyond[1], projected))
    total = (beyond[0].astype(F32) + far.astype(F32)).astype(BF)
    across = hop(total, 2)
    last_s = hop((skip_2 + got_s[1].astype(F32)).astype(BF), 2)
    arrived = exchange([after(piece, total) for piece in own_input], "shard", group)
    pair = jnp.stack([total, after(across, *arrived)])
    rest = hop(pair, 1)
    last_s = after(last_s, pair)
    sum_s = (skip_0 + got_s[0].astype(F32) + last_s.astype(F32)).astype(BF)
    beyond_s = sum_beyond_block(sum_s)
    input_grad = finish_images(after(ids, sum_s), arrived, chans)
    far_s = after(beyond_s[1], input_grad)
    full_s = (beyond_s[0].astype(F32) + far_s.astype(F32)).astype(BF)
    factor = 1.0 / math.sqrt(ranks * group * few)
    across_s = hop(full_s, 2)
    first = place_grad(after(ids, full_s), (0, 2), pair, own, chans, factor)
    pair_s = jnp.stack([full_s, after(across_s, first[0])])
    rest_s = hop(pair_s, 1)
    skip_grad = place_skip(
        ids, [((0, 2), pair_s), ((1, 3), rest_s)], own, wide, factor
    )
    rest = after(rest, skip_grad)
    conv_grad = place_grad(ids, (1, 3), rest, own, chans, factor, first)

    return (
        hidden.reshape(images.shape),
        projected,
        input_grad.reshape(images.shape),
        conv_grad,
        skip_grad,
    )


def solution(mesh):
    placed = (
        P(("rep", "shard"), None, None, None),
        P("shard", None),
        P("shard", None),
        P(("rep", "shard"), None, None, None),
        P(("rep", "shard"), None, None, None),
    )
    return jax.shard_map(
        on_device,
        mesh=mesh,
        in_specs=placed,
        out_specs=(
            P(("rep", "shard"), None, None, None),
            P(("rep", "shard"), None, None, None),
            P(("rep", "shard"), None, None, None),
            P("shard", None),
            P("shard", None),
        ),
        check_vma=False,
    )
```

```python
import math

import jax
import jax.numpy as jnp
from jax import lax
from jax.experimental import pallas as pl
from jax.experimental.pallas import tpu as pltpu
from jax.sharding import PartitionSpec as P

BF = jnp.bfloat16
F32 = jnp.float32
VMEM_LIMIT = 56 << 20
LANES = 128
BLOCK = 4


def dot(a, b, dims=((1,), (0,))):
    return lax.dot_general(a, b, (dims, ((), ())), preferred_element_type=F32)


NT = ((1,), (1,))
TN = ((0,), (0,))


def call(name, body, outs, scratch, flops, moved, args, scalars=0):
    specs = [
        pl.BlockSpec(memory_space=pltpu.SMEM if i < scalars else pltpu.VMEM)
        for i in range(len(args))
    ]
    return pl.pallas_call(
        body,
        out_shape=outs,
        in_specs=specs,
        out_specs=jax.tree.map(lambda _: pl.BlockSpec(memory_space=pltpu.VMEM), outs),
        scratch_shapes=scratch,
        compiler_params=pltpu.CompilerParams(vmem_limit_bytes=VMEM_LIMIT),
        cost_estimate=pl.CostEstimate(flops=flops, bytes_accessed=moved, transcendentals=0),
        name=name,
    )(*args)


def shape(dims, kind):
    return jax.ShapeDtypeStruct(dims, kind)


def rows_at(start, size, step):
    return pl.ds(pl.multiple_of(start, step), size)


def round_up(value, step):
    return -(-value // step) * step


def turn_filters(conv_weight):
    rows, chans = conv_weight.shape
    own = rows // 9

    def body(w_ref, o_ref, t_ref, wide):
        for k in range(chans // LANES):
            cols = slice(k * LANES, (k + 1) * LANES)
            wide[k] = w_ref[:, cols].astype(F32)
            for t in range(9):
                piece = wide[k, pl.ds(t, own, stride=9), :]
                o_ref[t * own : (t + 1) * own, cols] = piece.astype(BF)
        t_ref[...] = o_ref[...].T

    return call(
        "turn_filters",
        body,
        [shape((rows, chans), BF), shape((chans, rows), BF)],
        [pltpu.VMEM((chans // LANES, rows, LANES), F32)],
        0,
        6 * rows * chans,
        [conv_weight],
    )


def col_sets(chans):
    rest = (chans - BLOCK * LANES) // BLOCK
    return BLOCK * LANES, rest


def turn_images(ids, source, group, own):
    pixels, chans = source.shape

    def body(id_ref, i_ref, *refs):
        wide = refs[group]
        wide[...] = i_ref[...].astype(F32).T
        for j in range(group):
            refs[j][...] = wide[rows_at((id_ref[0] ^ j) * own, own, 8), :].astype(BF)

    return call(
        "turn_images",
        body,
        [shape((own, pixels), BF)] * group,
        [pltpu.VMEM((chans, pixels), F32)],
        0,
        4 * pixels * chans,
        [ids, source],
        1,
    )


def back_product(ids, cots, skip_weight):
    few, wide_chans = cots[0].shape
    own = skip_weight.shape[0]
    group = len(cots)

    def body(id_ref, s_ref, *refs):
        o_ref, held = refs[group:]
        for j in range(group):
            held[rows_at((id_ref[0] ^ j) * few, few, 16), :] = refs[j][...]
        o_ref[...] = dot(s_ref[...], held[...], NT).astype(BF)

    return call(
        "back_product",
        body,
        [shape((own, group * few), BF), shape((group * few, wide_chans), BF)],
        [],
        2 * own * group * few * wide_chans,
        group * few * wide_chans * 2,
        [ids, skip_weight, *cots],
        1,
    )


def pixel_parts(pixels, width):
    at = lax.broadcasted_iota(jnp.int32, (1, pixels), 1)
    return at // width, at % width


def neighbours(value, pixels, width):
    height = pixels // width
    y, x = pixel_parts(pixels, width)
    for dy in range(3):
        for dx in range(3):
            off = (dy - 1) * width + dx - 1
            if off == 0:
                yield value
                continue
            inside = (y >= 1 - dy) & (y < height + 1 - dy) & (x >= 1 - dx) & (x < width + 1 - dx)
            yield jnp.where(inside, pltpu.roll(value, -off % pixels, 1), 0.0)


def spread_matrix(few_all, few, pixels, width):
    y, x = pixel_parts(pixels, width)
    coarse = (y // 2) * (width // 2) + x // 2
    even = (y % 2 == 0) & (x % 2 == 0)
    row = lax.broadcasted_iota(jnp.int32, (few_all, pixels), 0)
    for d in range(few_all // few):
        yield jnp.where(even & (row == d * few + coarse), 1.0, 0.0).astype(BF)


def spread_rows(few_all, few, pixels, width, d):
    at = lax.broadcasted_iota(jnp.int32, (pixels, 1), 0)
    y, x = at // width, at % width
    coarse = jnp.where((y % 2 == 0) & (x % 2 == 0), (y // 2) * (width // 2) + x // 2, -few_all)
    col = lax.broadcasted_iota(jnp.int32, (pixels, few_all), 1)
    return jnp.where(col == d * few + coarse, 1.0, 0.0).astype(BF)


def make_patches(own_images, width):
    group = len(own_images)
    own, pixels = own_images[0].shape

    def body(*refs):
        patch = refs[group]
        for m in range(group):
            v = refs[m][...].astype(F32)
            value = (v / (1.0 + jnp.exp(-v))).astype(BF).astype(F32)
            here = slice(m * pixels, (m + 1) * pixels)
            for t, moved in enumerate(neighbours(value, pixels, width)):
                patch[t * own : (t + 1) * own, here] = moved.astype(BF)

    return call(
        "make_patches",
        body,
        shape((9 * own, group * pixels), BF),
        [],
        0,
        20 * own * group * pixels,
        own_images,
    )


def forward(ids, patch, w_turned, pixels, width, few):
    chans, rows = w_turned.shape
    group, own = patch.shape[1] // pixels, rows // 9
    few_all = group * few

    def body(id_ref, w_ref, p_ref, *refs):
        keep_refs = refs[: group // 2]
        send_ref, sums, moves = refs[group // 2 :]
        for m in range(group):
            here = slice(m * pixels, (m + 1) * pixels)
            moves[here] = spread_rows(few_all, few, pixels, width, id_ref[0] ^ m)
        out = dot(w_ref[...], p_ref[...])
        for m in range(group):
            piece = out[:, m * pixels : (m + 1) * pixels]
            if m % 2:
                send_ref[m // 2, :chans] = piece.astype(BF)
            else:
                keep_refs[m // 2][:chans] = piece
        evens = dot(p_ref[...], moves[...]).astype(BF)
        sums[...] = dot(w_ref[...], evens)
        for j in range(group):
            piece = sums[rows_at((id_ref[0] ^ j) * own, own, 8), :]
            for n in range(few_all // pixels):
                below = slice(chans + n * own, chans + (n + 1) * own)
                cols = piece[:, n * pixels : (n + 1) * pixels]
                if j % 2:
                    send_ref[j // 2, below] = cols.astype(BF)
                else:
                    keep_refs[j // 2][below] = cols

    return call(
        "forward",
        body,
        [shape((chans + own * few_all // pixels, pixels), F32)] * (group // 2)
        + [shape((group // 2, chans + own * few_all // pixels, pixels), BF)],
        [pltpu.VMEM((chans, few_all), F32), pltpu.VMEM((group * pixels, few_all), BF)],
        2 * group * pixels * rows * (chans + few_all),
        group * chans * pixels * 3,
        [ids, w_turned, patch],
        1,
    )


def filter_grad(ids, patch, hidden_cots, backs, width, few):
    rows = patch.shape[0]
    group = len(hidden_cots)
    pixels, chans = hidden_cots[0].shape
    own, few_all = backs[0].shape
    _, rest = col_sets(chans)
    tiles = chans // LANES
    part = round_up(-(-rows // BLOCK), 8)

    def body(id_ref, p_ref, *refs):
        cot_refs, back_refs = refs[:group], refs[group : 2 * group]
        hid = refs[2 * group]
        keep_refs, send_ref = refs[-5:-3], refs[-3]
        back, tile = refs[-2:]
        for j in range(group):
            back[rows_at((id_ref[0] ^ j) * own, own, 8), :] = back_refs[j][...].astype(F32)
        back_all = back[...].astype(BF)
        for j in range(group):
            d = id_ref[0] ^ j
            spread = dot(spread_rows(few_all, few, pixels, width, d), back_all, NT)
            hid[j * pixels : (j + 1) * pixels] = (cot_refs[j][...].astype(F32) + spread).astype(BF)
        total = dot(p_ref[...], hid[...])
        for n in range(tiles):
            tile[n] = total[:, n * LANES : (n + 1) * LANES]
        lane = lax.broadcasted_iota(jnp.int32, (part, LANES), 1) // rest
        for k in (1, 3, 0, 2):
            q = id_ref[1] ^ k
            share = jnp.zeros((part, LANES), F32)
            for i in range(BLOCK):
                size = min(part, rows - i * part)
                piece = tile[tiles - 1, i * part : i * part + size, :]
                if size < part:
                    piece = jnp.concatenate([piece, jnp.zeros((part - size, LANES), F32)])
                turn = ((i - q + BLOCK) % BLOCK) * rest
                share = share + jnp.where(lane == i, pltpu.roll(piece, turn, 1), 0.0)
            if k % 2:
                send_ref[k // 2, :rows] = tile[q].astype(BF)
                send_ref[k // 2, rows:] = share.astype(BF)
            else:
                keep_refs[k // 2][:rows] = tile[q]
                keep_refs[k // 2][rows:] = share

    return call(
        "filter_grad",
        body,
        [
            shape((group * pixels, chans), BF),
            shape((rows + part, LANES), F32),
            shape((rows + part, LANES), F32),
            shape((2, rows + part, LANES), BF),
        ],
        [
            pltpu.VMEM((chans, few_all), F32),
            pltpu.VMEM((tiles, rows, LANES), F32),
        ],
        2 * group * pixels * rows * chans,
        group * pixels * chans * 4 + rows * chans * 3,
        [ids, patch, *hidden_cots, *backs],
        1,
    )


def place_grad(ids, members, array, own, chans, scale, begun=None):
    rows = 9 * own
    part = round_up(-(-rows // BLOCK), 8)
    _, rest = col_sets(chans)
    tiles = chans // LANES
    final = begun is not None

    def body(id_ref, p_ref, *refs):
        if final:
            _, begun_ref, o_ref, wide, last, sems = refs
            last[...] = begun_ref[...]
        else:
            o_ref, last, wide, sems = refs
            last[...] = jnp.zeros_like(last)
        lane = lax.broadcasted_iota(jnp.int32, (part, LANES), 1) // rest

        def store(where, low, piece):
            high = low + piece.shape[0]
            for t in range(9):
                lo, hi = max(low, t * own), min(high, (t + 1) * own)
                if lo < hi:
                    wide[where, pl.ds((lo - t * own) * 9 + t, hi - lo, stride=9), :] = piece[
                        lo - low : hi - low
                    ]

        def copy_out(slot, where):
            at = pl.ds(pl.multiple_of(where * LANES, LANES), LANES)
            return pltpu.make_async_copy(wide.at[slot], o_ref.at[:, at], sems.at[slot])

        for n, k in enumerate(members):
            q = id_ref[1] ^ k
            store(n, 0, p_ref[n, :rows, :].astype(F32) * scale)
            copy_out(n, q).start()
            share = p_ref[n, rows:, :].astype(F32) * scale
            for i in range(BLOCK):
                turn = ((q - i + BLOCK) % BLOCK) * rest
                last[i] += jnp.where(lane == q, pltpu.roll(share, turn, 1), 0.0)
        if final:
            for i in range(BLOCK):
                store(2, i * part, last[i, : min(part, rows - i * part), :])
            copy_out(2, tiles - 1).start()
        for n, k in enumerate(members):
            copy_out(n, id_ref[1] ^ k).wait()
        if final:
            copy_out(2, tiles - 1).wait()

    vmem, anywhere = pl.BlockSpec(memory_space=pltpu.VMEM), pl.BlockSpec(memory_space=pl.ANY)
    share_shape = (BLOCK, part, LANES)
    scratch = [pltpu.VMEM((3, rows, LANES), F32)]
    if final:
        scratch.append(pltpu.VMEM(share_shape, F32))
    return pl.pallas_call(
        body,
        out_shape=shape((rows, chans), F32)
        if final
        else [shape((rows, chans), F32), shape(share_shape, F32)],
        in_specs=[pl.BlockSpec(memory_space=pltpu.SMEM), vmem] + [anywhere, vmem] * final,
        out_specs=anywhere if final else [anywhere, vmem],
        scratch_shapes=scratch + [pltpu.SemaphoreType.DMA((3,))],
        input_output_aliases={2: 0} if final else {},
        compiler_params=pltpu.CompilerParams(vmem_limit_bytes=VMEM_LIMIT),
        cost_estimate=pl.CostEstimate(
            flops=0, bytes_accessed=rows * chans * 3, transcendentals=0
        ),
        name="place_grad",
    )(ids, array, *(begun or ()))


def place_skip(ids, pieces, own, wide_chans, scale):
    few_rows = own // BLOCK

    def body(id_ref, *refs):
        o_ref, shares = refs[-2:]
        for ref, (members, _) in zip(refs, pieces):
            for n, k in enumerate(members):
                for i in range(wide_chans // LANES):
                    piece = ref[n, i * few_rows : (i + 1) * few_rows, :].astype(F32) * scale
                    shares[id_ref[1] ^ k, :, i * LANES : (i + 1) * LANES] = piece
        for q in range(BLOCK):
            o_ref[q * few_rows : (q + 1) * few_rows] = shares[q]

    return call(
        "place_skip",
        body,
        shape((own, wide_chans), F32),
        [pltpu.VMEM((BLOCK, few_rows, wide_chans), F32)],
        0,
        6 * own * wide_chans,
        [ids, *[array for _, array in pieces]],
        1,
    )


def finish_hidden(source, held, got, width):
    pixels, chans = source.shape
    few = pixels // 4

    def body(s_ref, k_ref, g_ref, o_ref, sub_ref):
        total = (k_ref[:chans] + g_ref[:chans].astype(F32)).T
        hidden = (s_ref[...].astype(F32) + total).astype(BF)
        o_ref[...] = hidden
        (one_hot,) = spread_matrix(few, few, pixels, width)
        sub_ref[...] = dot(one_hot, hidden).astype(BF)

    return call(
        "finish_hidden",
        body,
        [shape((pixels, chans), BF), shape((few, chans), BF)],
        [],
        2 * few * pixels * chans,
        pixels * chans * 10,
        [source, held, got],
    )


def skip_grad_term(ids, held, got, own_images, cots, width, few):
    group = len(own_images)
    own, pixels = own_images[0].shape
    few_all, wide_chans = cots.shape
    blocks = few_all // pixels
    low = held.shape[0] - own * blocks
    part, tiles = own // BLOCK, wide_chans // LANES

    def body(id_ref, k_ref, g_ref, c_ref, *refs):
        keep_refs, send_ref, total = refs[-4:-2], refs[-2], refs[-1]
        sub = k_ref[low:] + g_ref[low:].astype(F32)
        sub = jnp.concatenate([sub[n * own : (n + 1) * own] for n in range(blocks)], axis=1)
        row = lax.broadcasted_iota(jnp.int32, (few_all, pixels), 0) // few
        every = jnp.zeros((few_all, pixels), F32)
        for matrix in spread_matrix(few_all, few, pixels, width):
            every = every + matrix.astype(F32)
        for j in range(group):
            chosen = jnp.where(row == (id_ref[0] ^ j), every, 0.0).astype(BF)
            sub = sub + dot(refs[j][...], chosen, NT)
        term = dot(sub.astype(BF), c_ref[...])
        for q in range(BLOCK):
            total[q] = term[q * part : (q + 1) * part]
        for k in range(BLOCK):
            piece = total[id_ref[1] ^ k]
            ref = send_ref.at[k // 2] if k % 2 else keep_refs[k // 2]
            for n in range(tiles):
                cols = piece[:, n * LANES : (n + 1) * LANES]
                ref[n * part : (n + 1) * part] = cols.astype(ref.dtype)

    return call(
        "skip_grad_term",
        body,
        [shape((part * tiles, LANES), F32)] * 2 + [shape((2, part * tiles, LANES), BF)],
        [pltpu.VMEM((BLOCK, part, wide_chans), F32)],
        2 * own * few_all * wide_chans,
        own * wide_chans * 4,
        [ids, held, got, cots, *own_images],
        1,
    )


def project(ids, sub, skips):
    few, chans = sub.shape
    own, wide_chans = skips[0].shape
    group = len(skips)

    def body(id_ref, s_ref, *refs):
        o_ref, turned = refs[group:]
        turned[...] = s_ref[...].astype(F32).T
        total = jnp.zeros((few, wide_chans), F32)
        for j in range(group):
            rows = turned[rows_at((id_ref[0] ^ j) * own, own, 8), :].astype(BF)
            total = total + dot(rows, refs[j][...], TN)
        o_ref[...] = total.astype(BF)

    return call(
        "project",
        body,
        shape((few, wide_chans), BF),
        [pltpu.VMEM((chans, few), F32)],
        2 * few * chans * wide_chans,
        chans * wide_chans * 2,
        [ids, sub, *skips],
        1,
    )


def image_grad(ids, hidden_grad, own_images, w_tap, width):
    group = len(own_images)
    own, pixels = own_images[0].shape
    rows, chans = w_tap.shape
    height = pixels // width

    def body(id_ref, h_ref, w_ref, *refs):
        img_refs = refs[:group]
        o_refs, turned, tap = refs[group:-2], refs[-2], refs[-1]
        y, x = pixel_parts(pixels, width)
        for j in range(group):
            hid = h_ref[j * pixels : (j + 1) * pixels]
            turned[...] = hid.astype(F32).T
            tap[...] = dot(w_ref[...], hid, NT)
            side = tap[4 * own : 5 * own]
            for dy in range(3):
                for dx in range(3):
                    off = (dy - 1) * width + dx - 1
                    if off == 0:
                        continue
                    inside = (y >= dy - 1) & (y < height + dy - 1)
                    inside = inside & (x >= dx - 1) & (x < width + dx - 1)
                    t = 3 * dy + dx
                    moved = pltpu.roll(tap[t * own : (t + 1) * own], off % pixels, 1)
                    side = side + jnp.where(inside, moved, 0.0)
            v = img_refs[j][...].astype(F32)
            sig = 1.0 / (1.0 + jnp.exp(-v))
            slope = sig * (1.0 + v * (1.0 - sig))
            mine = turned[rows_at(id_ref[0] * own, own, 8), :]
            o_refs[j][...] = (mine + slope * side).astype(BF)

    return call(
        "image_grad",
        body,
        [shape((own, pixels), BF)] * group,
        [pltpu.VMEM((chans, pixels), F32), pltpu.VMEM((rows, pixels), F32)],
        2 * group * pixels * rows * chans,
        group * pixels * chans * 2,
        [ids, hidden_grad, w_tap, *own_images],
        1,
    )


def finish_images(ids, pieces, chans):
    group = len(pieces)
    own, pixels = pieces[0].shape

    def body(id_ref, *refs):
        o_ref, wide = refs[group:]
        for j in range(group):
            wide[rows_at((id_ref[0] ^ j) * own, own, 8), :] = refs[j][...].astype(F32)
        o_ref[...] = wide[...].T.astype(BF)

    return call(
        "finish_images",
        body,
        shape((pixels, chans), BF),
        [pltpu.VMEM((chans, pixels), F32)],
        0,
        pixels * chans * 4,
        [ids, *pieces],
        1,
    )


def flip(value, axis, bit):
    return lax.ppermute(value, axis, [(i, i ^ bit) for i in range(lax.axis_size(axis))])


def after(value, *others):
    return lax.optimization_barrier((value, *others))[0]


def high_bits(count):
    return [1 << k for k in reversed(range(count.bit_length() - 1))]


def gather(value, axis, *others):
    found = {0: value}
    for n, bit in enumerate(high_bits(lax.axis_size(axis))):
        for j, held in list(found.items()):
            if n == 1 and j and others:
                held = found[j] = after(held, *others)
            found[j ^ bit] = flip(held, axis, bit)
    return [found[j] for j in range(len(found))]


def exchange(blocks, axis, count):
    return [flip(blocks[j], axis, j) if j else blocks[0] for j in range(count)]


def hop(value, bit):
    ranks, group = lax.axis_size("rep"), lax.axis_size("shard")
    pairs = []
    for r in range(ranks):
        for s in range(group):
            other = r ^ (bit if s % 2 == 0 else 3 - bit)
            pairs.append((r * group + s, other * group + s))
    return lax.ppermute(value, ("rep", "shard"), pairs)


def sum_beyond_block(value):
    bits = [bit for bit in reversed(high_bits(lax.axis_size("rep"))) if bit >= BLOCK]
    got = jnp.zeros_like(value)
    for n, bit in enumerate(bits):
        if n:
            value = (value.astype(F32) + got.astype(F32)).astype(BF)
        got = flip(value, "rep", bit)
    return value, got


def add_beyond_block(value):
    value, got = sum_beyond_block(value)
    return (value.astype(F32) + got.astype(F32)).astype(BF)


def sum_scatter(keep, send):
    bits = list(reversed(high_bits(lax.axis_size("shard"))))
    for bit in bits[:-1]:
        got = flip(send, "shard", bit)
        total = [held + got[i].astype(F32) for i, held in enumerate(keep)]
        keep, send = total[0::2], jnp.stack(total[1::2]).astype(BF)
    return keep[0], send[0], flip(send[0], "shard", bits[-1])


def on_device(images, conv_weight, skip_weight, cotangent, hidden_cot):
    _, height, width, chans = images.shape
    own, wide = skip_weight.shape
    pixels, few = height * width, (height // 2) * (width // 2)
    group, ranks = lax.axis_size("shard"), lax.axis_size("rep")
    shard, rank = lax.axis_index("shard"), lax.axis_index("rep") % BLOCK
    member = jnp.where(shard % 2 == 0, rank, rank // 2 + 2 * (rank % 2))
    ids = jnp.stack([shard, member]).astype(jnp.int32)
    source = images.reshape(pixels, chans)

    img_sets = turn_images(ids, source, group, own)
    cots = gather(cotangent.reshape(few, wide), "shard", img_sets[0])
    own_images = exchange(img_sets, "shard", group)
    w_tap, w_turned = turn_filters(after(conv_weight, img_sets[0]))
    back, cots = back_product(after(ids, *own_images), cots, skip_weight)
    backs = [back] + [flip(back, "shard", j) for j in range(1, group)]
    patch = make_patches([after(piece, back) for piece in own_images], width)
    hidden_cots = hidden_cot.reshape(pixels, chans)
    hidden_cots = gather(after(hidden_cots, *own_images[2:], w_tap), "shard", patch, *backs)

    hidden_grad, keep_0, keep_2, send_g = filter_grad(
        after(ids, patch), patch, hidden_cots, backs, width, few
    )
    got_g = hop(send_g, 1)
    *keep, send = forward(after(ids, send_g), patch, w_turned, pixels, width, few)
    skips = gather(after(skip_weight, send_g), "shard")
    got_g = after(got_g, send, skips[2])
    mid_g = (keep_2 + got_g[1].astype(F32)).astype(BF)
    last_g = hop(mid_g, 2)
    keep, last, got = sum_scatter(keep, send)
    own_input = image_grad(after(ids, last), hidden_grad, own_images, w_tap, width)
    last_g = after(last_g, own_input[0], got, *skips)
    sum_g = (keep_0 + got_g[0].astype(F32) + last_g.astype(F32)).astype(BF)

    beyond = sum_beyond_block(sum_g)
    skip_0, skip_2, send_s = skip_grad_term(
        after(ids, sum_g), keep, got, own_images, cots, width, few
    )
    hidden, sub = finish_hidden(after(source, sum_g), keep, got, width)
    got_s = hop(send_s, 1)
    projected = project(ids, sub, skips).reshape(cotangent.shape)
    got_s, far, projected = lax.optimization_barrier((got_s, beyond[1], projected))
    total = (beyond[0].astype(F32) + far.astype(F32)).astype(BF)
    across = hop(total, 2)
    last_s = hop((skip_2 + got_s[1].astype(F32)).astype(BF), 2)
    arrived = exchange([after(piece, total) for piece in own_input], "shard", group)
    pair = jnp.stack([total, after(across, *arrived)])
    rest = hop(pair, 1)
    last_s = after(last_s, pair)
    sum_s = (skip_0 + got_s[0].astype(F32) + last_s.astype(F32)).astype(BF)
    beyond_s = sum_beyond_block(sum_s)
    input_grad = finish_images(after(ids, sum_s), arrived, chans)
    far_s = after(beyond_s[1], input_grad)
    full_s = (beyond_s[0].astype(F32) + far_s.astype(F32)).astype(BF)
    factor = 1.0 / math.sqrt(ranks * group * few)
    across_s = hop(full_s, 2)
    first = place_grad(after(ids, full_s), (0, 2), pair, own, chans, factor)
    pair_s = jnp.stack([full_s, after(across_s, first[0])])
    rest_s = hop(pair_s, 1)
    conv_grad = place_grad(ids, (1, 3), rest, own, chans, factor, first)
    rest_s = after(rest_s, conv_grad)
    skip_grad = place_skip(ids, [((0, 2), pair_s), ((1, 3), rest_s)], own, wide, factor)

    return (
        hidden.reshape(images.shape),
        projected,
        input_grad.reshape(images.shape),
        conv_grad,
        skip_grad,
    )


def solution(mesh):
    placed = (
        P(("rep", "shard"), None, None, None),
        P("shard", None),
        P("shard", None),
        P(("rep", "shard"), None, None, None),
        P(("rep", "shard"), None, None, None),
    )
    return jax.shard_map(
        on_device,
        mesh=mesh,
        in_specs=placed,
        out_specs=(
            P(("rep", "shard"), None, None, None),
            P(("rep", "shard"), None, None, None),
            P(("rep", "shard"), None, None, None),
            P("shard", None),
            P("shard", None),
        ),
        check_vma=False,
    )
```

```python
import math

import jax
import jax.numpy as jnp
from jax import lax
from jax.experimental import pallas as pl
from jax.experimental.pallas import tpu as pltpu
from jax.sharding import PartitionSpec as P

BF = jnp.bfloat16
F32 = jnp.float32
VMEM_LIMIT = 56 << 20
LANES = 128
BLOCK = 4


def dot(a, b, dims=((1,), (0,))):
    return lax.dot_general(a, b, (dims, ((), ())), preferred_element_type=F32)


NT = ((1,), (1,))
TN = ((0,), (0,))


def call(name, body, outs, scratch, flops, moved, args, scalars=0):
    specs = [
        pl.BlockSpec(memory_space=pltpu.SMEM if i < scalars else pltpu.VMEM)
        for i in range(len(args))
    ]
    return pl.pallas_call(
        body,
        out_shape=outs,
        in_specs=specs,
        out_specs=jax.tree.map(lambda _: pl.BlockSpec(memory_space=pltpu.VMEM), outs),
        scratch_shapes=scratch,
        compiler_params=pltpu.CompilerParams(vmem_limit_bytes=VMEM_LIMIT),
        cost_estimate=pl.CostEstimate(flops=flops, bytes_accessed=moved, transcendentals=0),
        name=name,
    )(*args)


def shape(dims, kind):
    return jax.ShapeDtypeStruct(dims, kind)


def rows_at(start, size, step):
    return pl.ds(pl.multiple_of(start, step), size)


def round_up(value, step):
    return -(-value // step) * step


def turn_filters(conv_weight):
    rows, chans = conv_weight.shape
    own = rows // 9

    def body(w_ref, o_ref, t_ref, wide):
        for k in range(chans // LANES):
            cols = slice(k * LANES, (k + 1) * LANES)
            wide[k] = w_ref[:, cols].astype(F32)
            for t in range(9):
                piece = wide[k, pl.ds(t, own, stride=9), :]
                o_ref[t * own : (t + 1) * own, cols] = piece.astype(BF)
        t_ref[...] = o_ref[...].T

    return call(
        "turn_filters",
        body,
        [shape((rows, chans), BF), shape((chans, rows), BF)],
        [pltpu.VMEM((chans // LANES, rows, LANES), F32)],
        0,
        6 * rows * chans,
        [conv_weight],
    )


def col_sets(chans):
    rest = (chans - BLOCK * LANES) // BLOCK
    return BLOCK * LANES, rest


def turn_images(ids, source, group, own):
    pixels, chans = source.shape

    def body(id_ref, i_ref, *refs):
        wide = refs[group]
        wide[...] = i_ref[...].astype(F32).T
        for j in range(group):
            refs[j][...] = wide[rows_at((id_ref[0] ^ j) * own, own, 8), :].astype(BF)

    return call(
        "turn_images",
        body,
        [shape((own, pixels), BF)] * group,
        [pltpu.VMEM((chans, pixels), F32)],
        0,
        4 * pixels * chans,
        [ids, source],
        1,
    )


def back_product(ids, cots, skip_weight):
    few, wide_chans = cots[0].shape
    own = skip_weight.shape[0]
    group = len(cots)

    def body(id_ref, s_ref, *refs):
        o_ref, held = refs[group:]
        for j in range(group):
            held[rows_at((id_ref[0] ^ j) * few, few, 16), :] = refs[j][...]
        o_ref[...] = dot(s_ref[...], held[...], NT).astype(BF)

    return call(
        "back_product",
        body,
        [shape((own, group * few), BF), shape((group * few, wide_chans), BF)],
        [],
        2 * own * group * few * wide_chans,
        group * few * wide_chans * 2,
        [ids, skip_weight, *cots],
        1,
    )


def pixel_parts(pixels, width):
    at = lax.broadcasted_iota(jnp.int32, (1, pixels), 1)
    return at // width, at % width


def neighbours(value, pixels, width):
    height = pixels // width
    y, x = pixel_parts(pixels, width)
    for dy in range(3):
        for dx in range(3):
            off = (dy - 1) * width + dx - 1
            if off == 0:
                yield value
                continue
            inside = (y >= 1 - dy) & (y < height + 1 - dy) & (x >= 1 - dx) & (x < width + 1 - dx)
            yield jnp.where(inside, pltpu.roll(value, -off % pixels, 1), 0.0)


def spread_matrix(few_all, few, pixels, width):
    y, x = pixel_parts(pixels, width)
    coarse = (y // 2) * (width // 2) + x // 2
    even = (y % 2 == 0) & (x % 2 == 0)
    row = lax.broadcasted_iota(jnp.int32, (few_all, pixels), 0)
    for d in range(few_all // few):
        yield jnp.where(even & (row == d * few + coarse), 1.0, 0.0).astype(BF)


def spread_rows(few_all, few, pixels, width, d):
    at = lax.broadcasted_iota(jnp.int32, (pixels, 1), 0)
    y, x = at // width, at % width
    coarse = jnp.where((y % 2 == 0) & (x % 2 == 0), (y // 2) * (width // 2) + x // 2, -few_all)
    col = lax.broadcasted_iota(jnp.int32, (pixels, few_all), 1)
    return jnp.where(col == d * few + coarse, 1.0, 0.0).astype(BF)


def make_patches(own_images, width):
    group = len(own_images)
    own, pixels = own_images[0].shape

    def body(*refs):
        patch = refs[group]
        for m in range(group):
            v = refs[m][...].astype(F32)
            value = (v / (1.0 + jnp.exp(-v))).astype(BF).astype(F32)
            here = slice(m * pixels, (m + 1) * pixels)
            for t, moved in enumerate(neighbours(value, pixels, width)):
                patch[t * own : (t + 1) * own, here] = moved.astype(BF)

    return call(
        "make_patches",
        body,
        shape((9 * own, group * pixels), BF),
        [],
        0,
        20 * own * group * pixels,
        own_images,
    )


def forward(ids, patch, w_turned, pixels, width, few):
    chans, rows = w_turned.shape
    group, own = patch.shape[1] // pixels, rows // 9
    few_all = group * few

    def body(id_ref, w_ref, p_ref, *refs):
        keep_refs = refs[: group // 2]
        send_ref, sums, moves = refs[group // 2 :]
        for m in range(group):
            here = slice(m * pixels, (m + 1) * pixels)
            moves[here] = spread_rows(few_all, few, pixels, width, id_ref[0] ^ m)
        out = dot(w_ref[...], p_ref[...])
        for m in range(group):
            piece = out[:, m * pixels : (m + 1) * pixels]
            if m % 2:
                send_ref[m // 2, :chans] = piece.astype(BF)
            else:
                keep_refs[m // 2][:chans] = piece
        evens = dot(p_ref[...], moves[...]).astype(BF)
        sums[...] = dot(w_ref[...], evens)
        for j in range(group):
            piece = sums[rows_at((id_ref[0] ^ j) * own, own, 8), :]
            for n in range(few_all // pixels):
                below = slice(chans + n * own, chans + (n + 1) * own)
                cols = piece[:, n * pixels : (n + 1) * pixels]
                if j % 2:
                    send_ref[j // 2, below] = cols.astype(BF)
                else:
                    keep_refs[j // 2][below] = cols

    return call(
        "forward",
        body,
        [shape((chans + own * few_all // pixels, pixels), F32)] * (group // 2)
        + [shape((group // 2, chans + own * few_all // pixels, pixels), BF)],
        [pltpu.VMEM((chans, few_all), F32), pltpu.VMEM((group * pixels, few_all), BF)],
        2 * group * pixels * rows * (chans + few_all),
        group * chans * pixels * 3,
        [ids, w_turned, patch],
        1,
    )


def filter_grad(ids, patch, hidden_cots, backs, width, few):
    rows = patch.shape[0]
    group = len(hidden_cots)
    pixels, chans = hidden_cots[0].shape
    own, few_all = backs[0].shape
    _, rest = col_sets(chans)
    tiles = chans // LANES
    part = round_up(-(-rows // BLOCK), 8)

    def body(id_ref, p_ref, *refs):
        cot_refs, back_refs = refs[:group], refs[group : 2 * group]
        hid = refs[2 * group]
        keep_refs, send_ref = refs[-5:-3], refs[-3]
        back, tile = refs[-2:]
        for j in range(group):
            back[rows_at((id_ref[0] ^ j) * own, own, 8), :] = back_refs[j][...].astype(F32)
        back_all = back[...].astype(BF)
        for j in range(group):
            d = id_ref[0] ^ j
            spread = dot(spread_rows(few_all, few, pixels, width, d), back_all, NT)
            hid[j * pixels : (j + 1) * pixels] = (cot_refs[j][...].astype(F32) + spread).astype(BF)
        total = dot(p_ref[...], hid[...])
        for n in range(tiles):
            tile[n] = total[:, n * LANES : (n + 1) * LANES]
        lane = lax.broadcasted_iota(jnp.int32, (part, LANES), 1) // rest
        for k in (1, 3, 0, 2):
            q = id_ref[1] ^ k
            share = jnp.zeros((part, LANES), F32)
            for i in range(BLOCK):
                size = min(part, rows - i * part)
                piece = tile[tiles - 1, i * part : i * part + size, :]
                if size < part:
                    piece = jnp.concatenate([piece, jnp.zeros((part - size, LANES), F32)])
                turn = ((i - q + BLOCK) % BLOCK) * rest
                share = share + jnp.where(lane == i, pltpu.roll(piece, turn, 1), 0.0)
            if k % 2:
                send_ref[k // 2, :rows] = tile[q].astype(BF)
                send_ref[k // 2, rows:] = share.astype(BF)
            else:
                keep_refs[k // 2][:rows] = tile[q]
                keep_refs[k // 2][rows:] = share

    return call(
        "filter_grad",
        body,
        [
            shape((group * pixels, chans), BF),
            shape((rows + part, LANES), F32),
            shape((rows + part, LANES), F32),
            shape((2, rows + part, LANES), BF),
        ],
        [
            pltpu.VMEM((chans, few_all), F32),
            pltpu.VMEM((tiles, rows, LANES), F32),
        ],
        2 * group * pixels * rows * chans,
        group * pixels * chans * 4 + rows * chans * 3,
        [ids, patch, *hidden_cots, *backs],
        1,
    )


def place_grad(ids, members, array, own, chans, scale, begun=None):
    rows = 9 * own
    part = round_up(-(-rows // BLOCK), 8)
    _, rest = col_sets(chans)
    tiles = chans // LANES
    final = begun is not None

    def body(id_ref, p_ref, *refs):
        if final:
            _, begun_ref, o_ref, wide, last, sems = refs
            last[...] = begun_ref[...]
        else:
            o_ref, last, wide, sems = refs
            last[...] = jnp.zeros_like(last)
        lane = lax.broadcasted_iota(jnp.int32, (part, LANES), 1) // rest

        def store(where, low, piece):
            high = low + piece.shape[0]
            for t in range(9):
                lo, hi = max(low, t * own), min(high, (t + 1) * own)
                if lo < hi:
                    wide[where, pl.ds((lo - t * own) * 9 + t, hi - lo, stride=9), :] = piece[
                        lo - low : hi - low
                    ]

        def copy_out(slot, where):
            at = pl.ds(pl.multiple_of(where * LANES, LANES), LANES)
            return pltpu.make_async_copy(wide.at[slot], o_ref.at[:, at], sems.at[slot])

        for n, k in enumerate(members):
            q = id_ref[1] ^ k
            store(n, 0, p_ref[n, :rows, :].astype(F32) * scale)
            copy_out(n, q).start()
            share = p_ref[n, rows:, :].astype(F32) * scale
            for i in range(BLOCK):
                turn = ((q - i + BLOCK) % BLOCK) * rest
                last[i] += jnp.where(lane == q, pltpu.roll(share, turn, 1), 0.0)
        if final:
            for i in range(BLOCK):
                store(2, i * part, last[i, : min(part, rows - i * part), :])
            copy_out(2, tiles - 1).start()
        for n, k in enumerate(members):
            copy_out(n, id_ref[1] ^ k).wait()
        if final:
            copy_out(2, tiles - 1).wait()

    vmem, anywhere = pl.BlockSpec(memory_space=pltpu.VMEM), pl.BlockSpec(memory_space=pl.ANY)
    share_shape = (BLOCK, part, LANES)
    scratch = [pltpu.VMEM((3, rows, LANES), F32)]
    if final:
        scratch.append(pltpu.VMEM(share_shape, F32))
    return pl.pallas_call(
        body,
        out_shape=shape((rows, chans), F32)
        if final
        else [shape((rows, chans), F32), shape(share_shape, F32)],
        in_specs=[pl.BlockSpec(memory_space=pltpu.SMEM), vmem] + [anywhere, vmem] * final,
        out_specs=anywhere if final else [anywhere, vmem],
        scratch_shapes=scratch + [pltpu.SemaphoreType.DMA((3,))],
        input_output_aliases={2: 0} if final else {},
        compiler_params=pltpu.CompilerParams(vmem_limit_bytes=VMEM_LIMIT),
        cost_estimate=pl.CostEstimate(
            flops=0, bytes_accessed=rows * chans * 3, transcendentals=0
        ),
        name="place_grad",
    )(ids, array, *(begun or ()))


def place_skip(ids, pieces, own, wide_chans, scale):
    few_rows = own // BLOCK

    def body(id_ref, *refs):
        o_ref, shares = refs[-2:]
        for ref, (members, _) in zip(refs, pieces):
            for n, k in enumerate(members):
                for i in range(wide_chans // LANES):
                    piece = ref[n, i * few_rows : (i + 1) * few_rows, :].astype(F32) * scale
                    shares[id_ref[1] ^ k, :, i * LANES : (i + 1) * LANES] = piece
        for q in range(BLOCK):
            o_ref[q * few_rows : (q + 1) * few_rows] = shares[q]

    return call(
        "place_skip",
        body,
        shape((own, wide_chans), F32),
        [pltpu.VMEM((BLOCK, few_rows, wide_chans), F32)],
        0,
        6 * own * wide_chans,
        [ids, *[array for _, array in pieces]],
        1,
    )


def finish_hidden(source, held, got, width):
    pixels, chans = source.shape
    few = pixels // 4

    def body(s_ref, k_ref, g_ref, o_ref, sub_ref):
        total = (k_ref[:chans] + g_ref[:chans].astype(F32)).T
        hidden = (s_ref[...].astype(F32) + total).astype(BF)
        o_ref[...] = hidden
        (one_hot,) = spread_matrix(few, few, pixels, width)
        sub_ref[...] = dot(one_hot, hidden).astype(BF)

    return call(
        "finish_hidden",
        body,
        [shape((pixels, chans), BF), shape((few, chans), BF)],
        [],
        2 * few * pixels * chans,
        pixels * chans * 10,
        [source, held, got],
    )


def skip_grad_term(ids, held, got, own_images, cots, width, few):
    group = len(own_images)
    own, pixels = own_images[0].shape
    few_all, wide_chans = cots.shape
    blocks = few_all // pixels
    low = held.shape[0] - own * blocks
    part, tiles = own // BLOCK, wide_chans // LANES

    def body(id_ref, k_ref, g_ref, c_ref, *refs):
        keep_refs, send_ref, total = refs[-4:-2], refs[-2], refs[-1]
        sub = k_ref[low:] + g_ref[low:].astype(F32)
        sub = jnp.concatenate([sub[n * own : (n + 1) * own] for n in range(blocks)], axis=1)
        row = lax.broadcasted_iota(jnp.int32, (few_all, pixels), 0) // few
        every = jnp.zeros((few_all, pixels), F32)
        for matrix in spread_matrix(few_all, few, pixels, width):
            every = every + matrix.astype(F32)
        for j in range(group):
            chosen = jnp.where(row == (id_ref[0] ^ j), every, 0.0).astype(BF)
            sub = sub + dot(refs[j][...], chosen, NT)
        term = dot(sub.astype(BF), c_ref[...])
        for q in range(BLOCK):
            total[q] = term[q * part : (q + 1) * part]
        for k in range(BLOCK):
            piece = total[id_ref[1] ^ k]
            ref = send_ref.at[k // 2] if k % 2 else keep_refs[k // 2]
            for n in range(tiles):
                cols = piece[:, n * LANES : (n + 1) * LANES]
                ref[n * part : (n + 1) * part] = cols.astype(ref.dtype)

    return call(
        "skip_grad_term",
        body,
        [shape((part * tiles, LANES), F32)] * 2 + [shape((2, part * tiles, LANES), BF)],
        [pltpu.VMEM((BLOCK, part, wide_chans), F32)],
        2 * own * few_all * wide_chans,
        own * wide_chans * 4,
        [ids, held, got, cots, *own_images],
        1,
    )


def project(ids, sub, skips):
    few, chans = sub.shape
    own, wide_chans = skips[0].shape
    group = len(skips)

    def body(id_ref, s_ref, *refs):
        o_ref, turned = refs[group:]
        turned[...] = s_ref[...].astype(F32).T
        total = jnp.zeros((few, wide_chans), F32)
        for j in range(group):
            rows = turned[rows_at((id_ref[0] ^ j) * own, own, 8), :].astype(BF)
            total = total + dot(rows, refs[j][...], TN)
        o_ref[...] = total.astype(BF)

    return call(
        "project",
        body,
        shape((few, wide_chans), BF),
        [pltpu.VMEM((chans, few), F32)],
        2 * few * chans * wide_chans,
        chans * wide_chans * 2,
        [ids, sub, *skips],
        1,
    )


def image_grad(ids, hidden_grad, own_images, w_tap, width):
    group = len(own_images)
    own, pixels = own_images[0].shape
    rows, chans = w_tap.shape
    height = pixels // width

    def body(id_ref, h_ref, w_ref, *refs):
        img_refs = refs[:group]
        o_refs, turned, tap = refs[group:-2], refs[-2], refs[-1]
        y, x = pixel_parts(pixels, width)
        for j in range(group):
            hid = h_ref[j * pixels : (j + 1) * pixels]
            turned[...] = hid.astype(F32).T
            tap[...] = dot(w_ref[...], hid, NT)
            side = tap[4 * own : 5 * own]
            for dy in range(3):
                for dx in range(3):
                    off = (dy - 1) * width + dx - 1
                    if off == 0:
                        continue
                    inside = (y >= dy - 1) & (y < height + dy - 1)
                    inside = inside & (x >= dx - 1) & (x < width + dx - 1)
                    t = 3 * dy + dx
                    moved = pltpu.roll(tap[t * own : (t + 1) * own], off % pixels, 1)
                    side = side + jnp.where(inside, moved, 0.0)
            v = img_refs[j][...].astype(F32)
            sig = 1.0 / (1.0 + jnp.exp(-v))
            slope = sig * (1.0 + v * (1.0 - sig))
            mine = turned[rows_at(id_ref[0] * own, own, 8), :]
            o_refs[j][...] = (mine + slope * side).astype(BF)

    return call(
        "image_grad",
        body,
        [shape((own, pixels), BF)] * group,
        [pltpu.VMEM((chans, pixels), F32), pltpu.VMEM((rows, pixels), F32)],
        2 * group * pixels * rows * chans,
        group * pixels * chans * 2,
        [ids, hidden_grad, w_tap, *own_images],
        1,
    )


def finish_images(ids, pieces, chans):
    group = len(pieces)
    own, pixels = pieces[0].shape

    def body(id_ref, *refs):
        o_ref, wide = refs[group:]
        for j in range(group):
            wide[rows_at((id_ref[0] ^ j) * own, own, 8), :] = refs[j][...].astype(F32)
        o_ref[...] = wide[...].T.astype(BF)

    return call(
        "finish_images",
        body,
        shape((pixels, chans), BF),
        [pltpu.VMEM((chans, pixels), F32)],
        0,
        pixels * chans * 4,
        [ids, *pieces],
        1,
    )


def flip(value, axis, bit):
    return lax.ppermute(value, axis, [(i, i ^ bit) for i in range(lax.axis_size(axis))])


def after(value, *others):
    return lax.optimization_barrier((value, *others))[0]


def high_bits(count):
    return [1 << k for k in reversed(range(count.bit_length() - 1))]


def gather(value, axis, *others):
    found = {0: value}
    for n, bit in enumerate(high_bits(lax.axis_size(axis))):
        for j, held in list(found.items()):
            if n == 1 and j and others:
                held = found[j] = after(held, *others)
            found[j ^ bit] = flip(held, axis, bit)
    return [found[j] for j in range(len(found))]


def exchange(blocks, axis, count):
    return [flip(blocks[j], axis, j) if j else blocks[0] for j in range(count)]


def hop(value, bit):
    ranks, group = lax.axis_size("rep"), lax.axis_size("shard")
    pairs = []
    for r in range(ranks):
        for s in range(group):
            other = r ^ (bit if s % 2 == 0 else 3 - bit)
            pairs.append((r * group + s, other * group + s))
    return lax.ppermute(value, ("rep", "shard"), pairs)


def sum_beyond_block(value):
    bits = [bit for bit in reversed(high_bits(lax.axis_size("rep"))) if bit >= BLOCK]
    got = jnp.zeros_like(value)
    for n, bit in enumerate(bits):
        if n:
            value = (value.astype(F32) + got.astype(F32)).astype(BF)
        got = flip(value, "rep", bit)
    return value, got


def add_beyond_block(value):
    value, got = sum_beyond_block(value)
    return (value.astype(F32) + got.astype(F32)).astype(BF)


def sum_scatter(keep, send):
    bits = list(reversed(high_bits(lax.axis_size("shard"))))
    for bit in bits[:-1]:
        got = flip(send, "shard", bit)
        total = [held + got[i].astype(F32) for i, held in enumerate(keep)]
        keep, send = total[0::2], jnp.stack(total[1::2]).astype(BF)
    return keep[0], send[0], flip(send[0], "shard", bits[-1])


def on_device(images, conv_weight, skip_weight, cotangent, hidden_cot):
    _, height, width, chans = images.shape
    own, wide = skip_weight.shape
    pixels, few = height * width, (height // 2) * (width // 2)
    group, ranks = lax.axis_size("shard"), lax.axis_size("rep")
    shard, rank = lax.axis_index("shard"), lax.axis_index("rep") % BLOCK
    member = jnp.where(shard % 2 == 0, rank, rank // 2 + 2 * (rank % 2))
    ids = jnp.stack([shard, member]).astype(jnp.int32)
    source = images.reshape(pixels, chans)

    img_sets = turn_images(ids, source, group, own)
    cots = gather(cotangent.reshape(few, wide), "shard", img_sets[0])
    own_images = exchange(img_sets, "shard", group)
    w_tap, w_turned = turn_filters(after(conv_weight, img_sets[0]))
    back, cots = back_product(after(ids, *own_images), cots, skip_weight)
    backs = [back] + [flip(back, "shard", j) for j in range(1, group)]
    patch = make_patches([after(piece, back) for piece in own_images], width)
    hidden_cots = hidden_cot.reshape(pixels, chans)
    hidden_cots = gather(after(hidden_cots, *own_images[2:], w_tap), "shard", patch, *backs)

    skips = gather(after(skip_weight, patch), "shard")

    hidden_grad, keep_0, keep_2, send_g = filter_grad(
        after(ids, patch), patch, hidden_cots, backs, width, few
    )
    got_g = hop(send_g, 1)
    *keep, send = forward(after(ids, send_g, skips[2]), patch, w_turned, pixels, width, few)
    got_g = after(got_g, send)
    mid_g = (keep_2 + got_g[1].astype(F32)).astype(BF)
    last_g = hop(mid_g, 2)
    keep, last, got = sum_scatter(keep, send)
    own_input = image_grad(after(ids, last), hidden_grad, own_images, w_tap, width)
    last_g = after(last_g, own_input[0], got, *skips)
    sum_g = (keep_0 + got_g[0].astype(F32) + last_g.astype(F32)).astype(BF)

    beyond = sum_beyond_block(sum_g)
    skip_0, skip_2, send_s = skip_grad_term(
        after(ids, sum_g), keep, got, own_images, cots, width, few
    )
    hidden, sub = finish_hidden(after(source, sum_g), keep, got, width)
    got_s = hop(send_s, 1)
    projected = project(ids, sub, skips).reshape(cotangent.shape)
    got_s, far, projected = lax.optimization_barrier((got_s, beyond[1], projected))
    total = (beyond[0].astype(F32) + far.astype(F32)).astype(BF)
    across = hop(total, 2)
    last_s = hop((skip_2 + got_s[1].astype(F32)).astype(BF), 2)
    arrived = exchange([after(piece, total) for piece in own_input], "shard", group)
    pair = jnp.stack([total, after(across, *arrived)])
    rest = hop(pair, 1)
    last_s = after(last_s, pair)
    sum_s = (skip_0 + got_s[0].astype(F32) + last_s.astype(F32)).astype(BF)
    beyond_s = sum_beyond_block(sum_s)
    input_grad = finish_images(after(ids, sum_s), arrived, chans)
    far_s = after(beyond_s[1], input_grad)
    full_s = (beyond_s[0].astype(F32) + far_s.astype(F32)).astype(BF)
    factor = 1.0 / math.sqrt(ranks * group * few)
    across_s = hop(full_s, 2)
    first = place_grad(after(ids, full_s), (0, 2), pair, own, chans, factor)
    pair_s = jnp.stack([full_s, after(across_s, first[0])])
    rest_s = hop(pair_s, 1)
    conv_grad = place_grad(ids, (1, 3), rest, own, chans, factor, first)
    rest_s = after(rest_s, conv_grad)
    skip_grad = place_skip(ids, [((0, 2), pair_s), ((1, 3), rest_s)], own, wide, factor)

    return (
        hidden.reshape(images.shape),
        projected,
        input_grad.reshape(images.shape),
        conv_grad,
        skip_grad,
    )


def solution(mesh):
    placed = (
        P(("rep", "shard"), None, None, None),
        P("shard", None),
        P("shard", None),
        P(("rep", "shard"), None, None, None),
        P(("rep", "shard"), None, None, None),
    )
    return jax.shard_map(
        on_device,
        mesh=mesh,
        in_specs=placed,
        out_specs=(
            P(("rep", "shard"), None, None, None),
            P(("rep", "shard"), None, None, None),
            P(("rep", "shard"), None, None, None),
            P("shard", None),
            P("shard", None),
        ),
        check_vma=False,
    )
```

```python
import math

import jax
import jax.numpy as jnp
from jax import lax
from jax.experimental import pallas as pl
from jax.experimental.pallas import tpu as pltpu
from jax.sharding import PartitionSpec as P

BF = jnp.bfloat16
F32 = jnp.float32
VMEM_LIMIT = 56 << 20
LANES = 128
BLOCK = 4


def dot(a, b, dims=((1,), (0,))):
    return lax.dot_general(a, b, (dims, ((), ())), preferred_element_type=F32)


NT = ((1,), (1,))
TN = ((0,), (0,))


def call(name, body, outs, scratch, flops, moved, args, scalars=0):
    specs = [
        pl.BlockSpec(memory_space=pltpu.SMEM if i < scalars else pltpu.VMEM)
        for i in range(len(args))
    ]
    return pl.pallas_call(
        body,
        out_shape=outs,
        in_specs=specs,
        out_specs=jax.tree.map(lambda _: pl.BlockSpec(memory_space=pltpu.VMEM), outs),
        scratch_shapes=scratch,
        compiler_params=pltpu.CompilerParams(vmem_limit_bytes=VMEM_LIMIT),
        cost_estimate=pl.CostEstimate(flops=flops, bytes_accessed=moved, transcendentals=0),
        name=name,
    )(*args)


def shape(dims, kind):
    return jax.ShapeDtypeStruct(dims, kind)


def rows_at(start, size, step):
    return pl.ds(pl.multiple_of(start, step), size)


def round_up(value, step):
    return -(-value // step) * step


def turn_filters(conv_weight):
    rows, chans = conv_weight.shape
    own = rows // 9

    def body(w_ref, o_ref, t_ref, wide):
        for k in range(chans // LANES):
            cols = slice(k * LANES, (k + 1) * LANES)
            wide[k] = w_ref[:, cols].astype(F32)
            for t in range(9):
                piece = wide[k, pl.ds(t, own, stride=9), :]
                o_ref[t * own : (t + 1) * own, cols] = piece.astype(BF)
        t_ref[...] = o_ref[...].T

    return call(
        "turn_filters",
        body,
        [shape((rows, chans), BF), shape((chans, rows), BF)],
        [pltpu.VMEM((chans // LANES, rows, LANES), F32)],
        0,
        6 * rows * chans,
        [conv_weight],
    )


def col_sets(chans):
    rest = (chans - BLOCK * LANES) // BLOCK
    return BLOCK * LANES, rest


def turn_images(ids, source, group, own):
    pixels, chans = source.shape

    def body(id_ref, i_ref, *refs):
        wide = refs[group]
        wide[...] = i_ref[...].astype(F32).T
        for j in range(group):
            refs[j][...] = wide[rows_at((id_ref[0] ^ j) * own, own, 8), :].astype(BF)

    return call(
        "turn_images",
        body,
        [shape((own, pixels), BF)] * group,
        [pltpu.VMEM((chans, pixels), F32)],
        0,
        4 * pixels * chans,
        [ids, source],
        1,
    )


def back_product(ids, cots, skip_weight):
    few, wide_chans = cots[0].shape
    own = skip_weight.shape[0]
    group = len(cots)

    def body(id_ref, s_ref, *refs):
        o_ref, held = refs[group:]
        for j in range(group):
            held[rows_at((id_ref[0] ^ j) * few, few, 16), :] = refs[j][...]
        o_ref[...] = dot(s_ref[...], held[...], NT).astype(BF)

    return call(
        "back_product",
        body,
        [shape((own, group * few), BF), shape((group * few, wide_chans), BF)],
        [],
        2 * own * group * few * wide_chans,
        group * few * wide_chans * 2,
        [ids, skip_weight, *cots],
        1,
    )


def pixel_parts(pixels, width):
    at = lax.broadcasted_iota(jnp.int32, (1, pixels), 1)
    return at // width, at % width


def neighbours(value, pixels, width):
    height = pixels // width
    y, x = pixel_parts(pixels, width)
    for dy in range(3):
        for dx in range(3):
            off = (dy - 1) * width + dx - 1
            if off == 0:
                yield value
                continue
            inside = (y >= 1 - dy) & (y < height + 1 - dy) & (x >= 1 - dx) & (x < width + 1 - dx)
            yield jnp.where(inside, pltpu.roll(value, -off % pixels, 1), 0.0)


def spread_matrix(few_all, few, pixels, width):
    y, x = pixel_parts(pixels, width)
    coarse = (y // 2) * (width // 2) + x // 2
    even = (y % 2 == 0) & (x % 2 == 0)
    row = lax.broadcasted_iota(jnp.int32, (few_all, pixels), 0)
    for d in range(few_all // few):
        yield jnp.where(even & (row == d * few + coarse), 1.0, 0.0).astype(BF)


def spread_rows(few_all, few, pixels, width, d):
    at = lax.broadcasted_iota(jnp.int32, (pixels, 1), 0)
    y, x = at // width, at % width
    coarse = jnp.where((y % 2 == 0) & (x % 2 == 0), (y // 2) * (width // 2) + x // 2, -few_all)
    col = lax.broadcasted_iota(jnp.int32, (pixels, few_all), 1)
    return jnp.where(col == d * few + coarse, 1.0, 0.0).astype(BF)


def make_patches(own_images, width):
    group = len(own_images)
    own, pixels = own_images[0].shape

    def body(*refs):
        patch = refs[group]
        for m in range(group):
            v = refs[m][...].astype(F32)
            value = (v / (1.0 + jnp.exp(-v))).astype(BF).astype(F32)
            here = slice(m * pixels, (m + 1) * pixels)
            for t, moved in enumerate(neighbours(value, pixels, width)):
                patch[t * own : (t + 1) * own, here] = moved.astype(BF)

    return call(
        "make_patches",
        body,
        shape((9 * own, group * pixels), BF),
        [],
        0,
        20 * own * group * pixels,
        own_images,
    )


def forward(ids, patch, w_turned, pixels, width, few):
    chans, rows = w_turned.shape
    group, own = patch.shape[1] // pixels, rows // 9
    few_all = group * few

    def body(id_ref, w_ref, p_ref, *refs):
        keep_refs = refs[: group // 2]
        send_ref, sums, moves = refs[group // 2 :]
        for m in range(group):
            here = slice(m * pixels, (m + 1) * pixels)
            moves[here] = spread_rows(few_all, few, pixels, width, id_ref[0] ^ m)
        out = dot(w_ref[...], p_ref[...])
        for m in range(group):
            piece = out[:, m * pixels : (m + 1) * pixels]
            if m % 2:
                send_ref[m // 2, :chans] = piece.astype(BF)
            else:
                keep_refs[m // 2][:chans] = piece
        evens = dot(p_ref[...], moves[...]).astype(BF)
        sums[...] = dot(w_ref[...], evens)
        for j in range(group):
            piece = sums[rows_at((id_ref[0] ^ j) * own, own, 8), :]
            for n in range(few_all // pixels):
                below = slice(chans + n * own, chans + (n + 1) * own)
                cols = piece[:, n * pixels : (n + 1) * pixels]
                if j % 2:
                    send_ref[j // 2, below] = cols.astype(BF)
                else:
                    keep_refs[j // 2][below] = cols

    return call(
        "forward",
        body,
        [shape((chans + own * few_all // pixels, pixels), F32)] * (group // 2)
        + [shape((group // 2, chans + own * few_all // pixels, pixels), BF)],
        [pltpu.VMEM((chans, few_all), F32), pltpu.VMEM((group * pixels, few_all), BF)],
        2 * group * pixels * rows * (chans + few_all),
        group * chans * pixels * 3,
        [ids, w_turned, patch],
        1,
    )


def filter_grad(ids, patch, hidden_cots, backs, width, few):
    rows = patch.shape[0]
    group = len(hidden_cots)
    pixels, chans = hidden_cots[0].shape
    own, few_all = backs[0].shape
    _, rest = col_sets(chans)
    tiles = chans // LANES
    part = round_up(-(-rows // BLOCK), 8)

    def body(id_ref, p_ref, *refs):
        cot_refs, back_refs = refs[:group], refs[group : 2 * group]
        hid = refs[2 * group]
        keep_refs, send_ref = refs[-5:-3], refs[-3]
        back, tile = refs[-2:]
        for j in range(group):
            back[rows_at((id_ref[0] ^ j) * own, own, 8), :] = back_refs[j][...].astype(F32)
        back_all = back[...].astype(BF)
        for j in range(group):
            d = id_ref[0] ^ j
            spread = dot(spread_rows(few_all, few, pixels, width, d), back_all, NT)
            hid[j * pixels : (j + 1) * pixels] = (cot_refs[j][...].astype(F32) + spread).astype(BF)
        total = dot(p_ref[...], hid[...])
        for n in range(tiles):
            tile[n] = total[:, n * LANES : (n + 1) * LANES]
        lane = lax.broadcasted_iota(jnp.int32, (part, LANES), 1) // rest
        for k in (1, 3, 0, 2):
            q = id_ref[1] ^ k
            share = jnp.zeros((part, LANES), F32)
            for i in range(BLOCK):
                size = min(part, rows - i * part)
                piece = tile[tiles - 1, i * part : i * part + size, :]
                if size < part:
                    piece = jnp.concatenate([piece, jnp.zeros((part - size, LANES), F32)])
                turn = ((i - q + BLOCK) % BLOCK) * rest
                share = share + jnp.where(lane == i, pltpu.roll(piece, turn, 1), 0.0)
            if k % 2:
                send_ref[k // 2, :rows] = tile[q].astype(BF)
                send_ref[k // 2, rows:] = share.astype(BF)
            else:
                keep_refs[k // 2][:rows] = tile[q]
                keep_refs[k // 2][rows:] = share

    return call(
        "filter_grad",
        body,
        [
            shape((group * pixels, chans), BF),
            shape((rows + part, LANES), F32),
            shape((rows + part, LANES), F32),
            shape((2, rows + part, LANES), BF),
        ],
        [
            pltpu.VMEM((chans, few_all), F32),
            pltpu.VMEM((tiles, rows, LANES), F32),
        ],
        2 * group * pixels * rows * chans,
        group * pixels * chans * 4 + rows * chans * 3,
        [ids, patch, *hidden_cots, *backs],
        1,
    )


def place_grad(ids, members, array, own, chans, scale, begun=None):
    rows = 9 * own
    part = round_up(-(-rows // BLOCK), 8)
    _, rest = col_sets(chans)
    tiles = chans // LANES
    final = begun is not None

    def body(id_ref, p_ref, *refs):
        if final:
            _, begun_ref, o_ref, wide, last, sems = refs
            last[...] = begun_ref[...]
        else:
            o_ref, last, wide, sems = refs
            last[...] = jnp.zeros_like(last)
        lane = lax.broadcasted_iota(jnp.int32, (part, LANES), 1) // rest

        def store(where, low, piece):
            high = low + piece.shape[0]
            for t in range(9):
                lo, hi = max(low, t * own), min(high, (t + 1) * own)
                if lo < hi:
                    wide[where, pl.ds((lo - t * own) * 9 + t, hi - lo, stride=9), :] = piece[
                        lo - low : hi - low
                    ]

        def copy_out(slot, where):
            at = pl.ds(pl.multiple_of(where * LANES, LANES), LANES)
            return pltpu.make_async_copy(wide.at[slot], o_ref.at[:, at], sems.at[slot])

        for n, k in enumerate(members):
            q = id_ref[1] ^ k
            store(n, 0, p_ref[n, :rows, :].astype(F32) * scale)
            copy_out(n, q).start()
            share = p_ref[n, rows:, :].astype(F32) * scale
            for i in range(BLOCK):
                turn = ((q - i + BLOCK) % BLOCK) * rest
                last[i] += jnp.where(lane == q, pltpu.roll(share, turn, 1), 0.0)
        if final:
            for i in range(BLOCK):
                store(2, i * part, last[i, : min(part, rows - i * part), :])
            copy_out(2, tiles - 1).start()
        for n, k in enumerate(members):
            copy_out(n, id_ref[1] ^ k).wait()
        if final:
            copy_out(2, tiles - 1).wait()

    vmem, anywhere = pl.BlockSpec(memory_space=pltpu.VMEM), pl.BlockSpec(memory_space=pl.ANY)
    share_shape = (BLOCK, part, LANES)
    scratch = [pltpu.VMEM((3, rows, LANES), F32)]
    if final:
        scratch.append(pltpu.VMEM(share_shape, F32))
    return pl.pallas_call(
        body,
        out_shape=shape((rows, chans), F32)
        if final
        else [shape((rows, chans), F32), shape(share_shape, F32)],
        in_specs=[pl.BlockSpec(memory_space=pltpu.SMEM), vmem] + [anywhere, vmem] * final,
        out_specs=anywhere if final else [anywhere, vmem],
        scratch_shapes=scratch + [pltpu.SemaphoreType.DMA((3,))],
        input_output_aliases={2: 0} if final else {},
        compiler_params=pltpu.CompilerParams(vmem_limit_bytes=VMEM_LIMIT),
        cost_estimate=pl.CostEstimate(
            flops=0, bytes_accessed=rows * chans * 3, transcendentals=0
        ),
        name="place_grad",
    )(ids, array, *(begun or ()))


def place_skip(ids, pieces, own, wide_chans, scale):
    few_rows = own // BLOCK

    def body(id_ref, *refs):
        o_ref, shares = refs[-2:]
        for ref, (members, _) in zip(refs, pieces):
            for n, k in enumerate(members):
                for i in range(wide_chans // LANES):
                    piece = ref[n, i * few_rows : (i + 1) * few_rows, :].astype(F32) * scale
                    shares[id_ref[1] ^ k, :, i * LANES : (i + 1) * LANES] = piece
        for q in range(BLOCK):
            o_ref[q * few_rows : (q + 1) * few_rows] = shares[q]

    return call(
        "place_skip",
        body,
        shape((own, wide_chans), F32),
        [pltpu.VMEM((BLOCK, few_rows, wide_chans), F32)],
        0,
        6 * own * wide_chans,
        [ids, *[array for _, array in pieces]],
        1,
    )


def finish_hidden(source, held, got, width):
    pixels, chans = source.shape
    few = pixels // 4

    def body(s_ref, k_ref, g_ref, o_ref, sub_ref):
        total = (k_ref[:chans] + g_ref[:chans].astype(F32)).T
        hidden = (s_ref[...].astype(F32) + total).astype(BF)
        o_ref[...] = hidden
        (one_hot,) = spread_matrix(few, few, pixels, width)
        sub_ref[...] = dot(one_hot, hidden).astype(BF)

    return call(
        "finish_hidden",
        body,
        [shape((pixels, chans), BF), shape((few, chans), BF)],
        [],
        2 * few * pixels * chans,
        pixels * chans * 10,
        [source, held, got],
    )


def skip_grad_term(ids, held, got, own_images, cots, width, few):
    group = len(own_images)
    own, pixels = own_images[0].shape
    few_all, wide_chans = cots.shape
    blocks = few_all // pixels
    low = held.shape[0] - own * blocks
    part, tiles = own // BLOCK, wide_chans // LANES

    def body(id_ref, k_ref, g_ref, c_ref, *refs):
        keep_refs, send_ref, total = refs[-4:-2], refs[-2], refs[-1]
        sub = k_ref[low:] + g_ref[low:].astype(F32)
        sub = jnp.concatenate([sub[n * own : (n + 1) * own] for n in range(blocks)], axis=1)
        row = lax.broadcasted_iota(jnp.int32, (few_all, pixels), 0) // few
        every = jnp.zeros((few_all, pixels), F32)
        for matrix in spread_matrix(few_all, few, pixels, width):
            every = every + matrix.astype(F32)
        for j in range(group):
            chosen = jnp.where(row == (id_ref[0] ^ j), every, 0.0).astype(BF)
            sub = sub + dot(refs[j][...], chosen, NT)
        term = dot(sub.astype(BF), c_ref[...])
        for q in range(BLOCK):
            total[q] = term[q * part : (q + 1) * part]
        for k in range(BLOCK):
            piece = total[id_ref[1] ^ k]
            ref = send_ref.at[k // 2] if k % 2 else keep_refs[k // 2]
            for n in range(tiles):
                cols = piece[:, n * LANES : (n + 1) * LANES]
                ref[n * part : (n + 1) * part] = cols.astype(ref.dtype)

    return call(
        "skip_grad_term",
        body,
        [shape((part * tiles, LANES), F32)] * 2 + [shape((2, part * tiles, LANES), BF)],
        [pltpu.VMEM((BLOCK, part, wide_chans), F32)],
        2 * own * few_all * wide_chans,
        own * wide_chans * 4,
        [ids, held, got, cots, *own_images],
        1,
    )


def project(ids, sub, skips):
    few, chans = sub.shape
    own, wide_chans = skips[0].shape
    group = len(skips)

    def body(id_ref, s_ref, *refs):
        o_ref, turned = refs[group:]
        turned[...] = s_ref[...].astype(F32).T
        total = jnp.zeros((few, wide_chans), F32)
        for j in range(group):
            rows = turned[rows_at((id_ref[0] ^ j) * own, own, 8), :].astype(BF)
            total = total + dot(rows, refs[j][...], TN)
        o_ref[...] = total.astype(BF)

    return call(
        "project",
        body,
        shape((few, wide_chans), BF),
        [pltpu.VMEM((chans, few), F32)],
        2 * few * chans * wide_chans,
        chans * wide_chans * 2,
        [ids, sub, *skips],
        1,
    )


def image_grad(ids, hidden_grad, own_images, w_tap, width):
    group = len(own_images)
    own, pixels = own_images[0].shape
    rows, chans = w_tap.shape
    height = pixels // width

    def body(id_ref, h_ref, w_ref, *refs):
        img_refs = refs[:group]
        o_refs, turned, tap = refs[group:-2], refs[-2], refs[-1]
        y, x = pixel_parts(pixels, width)
        for j in range(group):
            hid = h_ref[j * pixels : (j + 1) * pixels]
            turned[...] = hid.astype(F32).T
            tap[...] = dot(w_ref[...], hid, NT)
            side = tap[4 * own : 5 * own]
            for dy in range(3):
                for dx in range(3):
                    off = (dy - 1) * width + dx - 1
                    if off == 0:
                        continue
                    inside = (y >= dy - 1) & (y < height + dy - 1)
                    inside = inside & (x >= dx - 1) & (x < width + dx - 1)
                    t = 3 * dy + dx
                    moved = pltpu.roll(tap[t * own : (t + 1) * own], off % pixels, 1)
                    side = side + jnp.where(inside, moved, 0.0)
            v = img_refs[j][...].astype(F32)
            sig = 1.0 / (1.0 + jnp.exp(-v))
            slope = sig * (1.0 + v * (1.0 - sig))
            mine = turned[rows_at(id_ref[0] * own, own, 8), :]
            o_refs[j][...] = (mine + slope * side).astype(BF)

    return call(
        "image_grad",
        body,
        [shape((own, pixels), BF)] * group,
        [pltpu.VMEM((chans, pixels), F32), pltpu.VMEM((rows, pixels), F32)],
        2 * group * pixels * rows * chans,
        group * pixels * chans * 2,
        [ids, hidden_grad, w_tap, *own_images],
        1,
    )


def finish_images(ids, pieces, chans):
    group = len(pieces)
    own, pixels = pieces[0].shape

    def body(id_ref, *refs):
        o_ref, wide = refs[group:]
        for j in range(group):
            wide[rows_at((id_ref[0] ^ j) * own, own, 8), :] = refs[j][...].astype(F32)
        o_ref[...] = wide[...].T.astype(BF)

    return call(
        "finish_images",
        body,
        shape((pixels, chans), BF),
        [pltpu.VMEM((chans, pixels), F32)],
        0,
        pixels * chans * 4,
        [ids, *pieces],
        1,
    )


def flip(value, axis, bit):
    return lax.ppermute(value, axis, [(i, i ^ bit) for i in range(lax.axis_size(axis))])


def after(value, *others):
    return lax.optimization_barrier((value, *others))[0]


def high_bits(count):
    return [1 << k for k in reversed(range(count.bit_length() - 1))]


def gather(value, axis, *others):
    found = {0: value}
    for n, bit in enumerate(high_bits(lax.axis_size(axis))):
        for j, held in list(found.items()):
            if n == 1 and j and others:
                held = found[j] = after(held, *others)
            found[j ^ bit] = flip(held, axis, bit)
    return [found[j] for j in range(len(found))]


def exchange(blocks, axis, count):
    return [flip(blocks[j], axis, j) if j else blocks[0] for j in range(count)]


def hop(value, bit):
    ranks, group = lax.axis_size("rep"), lax.axis_size("shard")
    pairs = []
    for r in range(ranks):
        for s in range(group):
            other = r ^ (bit if s % 2 == 0 else 3 - bit)
            pairs.append((r * group + s, other * group + s))
    return lax.ppermute(value, ("rep", "shard"), pairs)


def sum_beyond_block(value):
    bits = [bit for bit in reversed(high_bits(lax.axis_size("rep"))) if bit >= BLOCK]
    got = jnp.zeros_like(value)
    for n, bit in enumerate(bits):
        if n:
            value = (value.astype(F32) + got.astype(F32)).astype(BF)
        got = flip(value, "rep", bit)
    return value, got


def add_beyond_block(value):
    value, got = sum_beyond_block(value)
    return (value.astype(F32) + got.astype(F32)).astype(BF)


def sum_scatter(keep, send):
    bits = list(reversed(high_bits(lax.axis_size("shard"))))
    for bit in bits[:-1]:
        got = flip(send, "shard", bit)
        total = [held + got[i].astype(F32) for i, held in enumerate(keep)]
        keep, send = total[0::2], jnp.stack(total[1::2]).astype(BF)
    return keep[0], send[0], flip(send[0], "shard", bits[-1])


def on_device(images, conv_weight, skip_weight, cotangent, hidden_cot):
    _, height, width, chans = images.shape
    own, wide = skip_weight.shape
    pixels, few = height * width, (height // 2) * (width // 2)
    group, ranks = lax.axis_size("shard"), lax.axis_size("rep")
    shard, rank = lax.axis_index("shard"), lax.axis_index("rep") % BLOCK
    member = jnp.where(shard % 2 == 0, rank, rank // 2 + 2 * (rank % 2))
    ids = jnp.stack([shard, member]).astype(jnp.int32)
    source = images.reshape(pixels, chans)

    img_sets = turn_images(ids, source, group, own)
    cots = gather(cotangent.reshape(few, wide), "shard", img_sets[0])
    own_images = exchange(img_sets, "shard", group)
    w_tap, w_turned = turn_filters(after(conv_weight, img_sets[0]))
    back, cots = back_product(after(ids, *own_images), cots, skip_weight)
    backs = [back] + [flip(back, "shard", j) for j in range(1, group)]
    patch = make_patches([after(piece, back) for piece in own_images], width)
    hidden_cots = hidden_cot.reshape(pixels, chans)
    hidden_cots = gather(after(hidden_cots, *own_images[2:], w_tap), "shard", patch, *backs)

    skips = gather(after(skip_weight, patch), "shard")

    hidden_grad, keep_0, keep_2, send_g = filter_grad(
        after(ids, patch), patch, hidden_cots, backs, width, few
    )
    got_g = hop(send_g, 1)
    *keep, send = forward(after(ids, send_g, skips[2]), patch, w_turned, pixels, width, few)
    got_g = after(got_g, send)
    mid_g = (keep_2 + got_g[1].astype(F32)).astype(BF)
    last_g = hop(mid_g, 2)
    keep, last, got = sum_scatter(keep, send)
    own_input = image_grad(after(ids, last), hidden_grad, own_images, w_tap, width)
    last_g = after(last_g, own_input[0], *skips)
    sum_g = (keep_0 + got_g[0].astype(F32) + last_g.astype(F32)).astype(BF)

    beyond = sum_beyond_block(sum_g)
    skip_0, skip_2, send_s = skip_grad_term(
        after(ids, sum_g), keep, got, own_images, cots, width, few
    )
    hidden, sub = finish_hidden(after(source, sum_g), keep, got, width)
    got_s = hop(send_s, 1)
    projected = project(ids, sub, skips).reshape(cotangent.shape)
    got_s, far, projected = lax.optimization_barrier((got_s, beyond[1], projected))
    total = (beyond[0].astype(F32) + far.astype(F32)).astype(BF)
    across = hop(total, 2)
    last_s = hop((skip_2 + got_s[1].astype(F32)).astype(BF), 2)
    arrived = exchange([after(piece, total) for piece in own_input], "shard", group)
    pair = jnp.stack([total, after(across, *arrived)])
    rest = hop(pair, 1)
    last_s = after(last_s, pair)
    sum_s = (skip_0 + got_s[0].astype(F32) + last_s.astype(F32)).astype(BF)
    beyond_s = sum_beyond_block(sum_s)
    input_grad = finish_images(after(ids, sum_s), arrived, chans)
    far_s = after(beyond_s[1], input_grad)
    full_s = (beyond_s[0].astype(F32) + far_s.astype(F32)).astype(BF)
    factor = 1.0 / math.sqrt(ranks * group * few)
    across_s = hop(full_s, 2)
    first = place_grad(after(ids, full_s), (0, 2), pair, own, chans, factor)
    pair_s = jnp.stack([full_s, after(across_s, first[0])])
    rest_s = hop(pair_s, 1)
    conv_grad = place_grad(ids, (1, 3), rest, own, chans, factor, first)
    rest_s = after(rest_s, conv_grad)
    skip_grad = place_skip(ids, [((0, 2), pair_s), ((1, 3), rest_s)], own, wide, factor)

    return (
        hidden.reshape(images.shape),
        projected,
        input_grad.reshape(images.shape),
        conv_grad,
        skip_grad,
    )


def solution(mesh):
    placed = (
        P(("rep", "shard"), None, None, None),
        P("shard", None),
        P("shard", None),
        P(("rep", "shard"), None, None, None),
        P(("rep", "shard"), None, None, None),
    )
    return jax.shard_map(
        on_device,
        mesh=mesh,
        in_specs=placed,
        out_specs=(
            P(("rep", "shard"), None, None, None),
            P(("rep", "shard"), None, None, None),
            P(("rep", "shard"), None, None, None),
            P("shard", None),
            P("shard", None),
        ),
        check_vma=False,
    )
```
